32 devices in a mesh: dp: 16 (over z, y, x), ctx: 2 (over core).
Axes of the slice: x: 2, y: 2, z: 4, core: 2. Of those that a mesh axis runs over, the one named last changes fastest.
Arguments:
- inputs: bfloat16 [16, 256, 4096], P('dp', 'ctx'), may hold values from -6 to 6
- cotangent: bfloat16 [16, 256, 4096], P('dp', 'ctx'), may hold values from -6 to 6
- segment_ids: int32 [16, 256], P('dp'), may hold values from 0 to 3, never falling along the last dimension, each value on 1 to 128 neighbouring positions
- taps: bfloat16 [4096, 128], replicated, may hold values from -0.5 to 0.5
- skip_gain: float32 [4096], replicated, may hold values from 0.5 to 2
Outputs:
- input_grad: bfloat16 [16, 256, 4096], P('dp', 'ctx')
- taps_grad: float32 [4096, 128], P('ctx')
- skip_grad: float32 [4096], P('ctx')
The draws below stay inside these ranges and needn't reach their ends.
Inputs may be any that keep to these rules, and one draw needn't show every extreme that they name: `segment_ids`: document numbers of a sequence never fall; each document has 1 to 128 positions, one exactly 128.
All inputs are finite; a program needn't handle non-finite values.
Results may differ from the reference program's by a relative error of at most 0.001.
Values may be sent and summed in bfloat16 or wider, within the bound.
No kernel may reach another device: no remote copies, remote signals or barrier semaphores. Data moves between devices by JAX's collectives and lax.ppermute only.
A program may use at most 128 MiB of HBM per device.

```python
import math
import jax
import jax.numpy as jnp
import numpy as np
from jax import lax

CH = 4096
TAPS = 128
DOCS = 4
LEN = 256
SEQS = 16
DOC_MOST = 128


def strengthened(drawn, stream_key, source, target, blocks, factor):
    owner, partner = [(jnp.arange(drawn.shape[dim]) // (drawn.shape[dim] // blocks)).reshape([-1 if axis == dim else 1 for axis in range(drawn.ndim)]) for dim in (source, target)]
    chosen = jax.random.permutation(stream_key, blocks)[partner]
    strong = (owner == chosen) | (owner == (partner + blocks // 2) % blocks)
    return jnp.where(strong, factor * drawn, drawn)


def level_of(stream_key, dims, shards, smallest, high):
    gain = 1.0
    for axis_at, parts in shards:
        heights = jax.random.uniform(jax.random.fold_in(jax.random.fold_in(stream_key, 6), axis_at), (parts,), jnp.float32, smallest / len(shards), high / len(shards))
        gain = gain * jnp.repeat(jnp.exp(heights), dims[axis_at] // parts).reshape((-1,) + (1,) * (len(dims) - 1 - axis_at))
    return gain


def split_up(number_of, total, bound, lean):
    loads = [(1 << 20) // math.isqrt(grade ** lean) + 1 for grade in range(2, number_of + 1)]
    rest, counts = total - bound - (number_of - 1), [1] * (number_of - 1)
    while rest > 0:
        candidates = [i for i in range(number_of - 1) if counts[i] < bound]
        whole, left = sum([loads[i] for i in candidates]), rest
        for i in candidates:
            addition = min(bound - counts[i], max(1, left * loads[i] // whole), rest)
            counts[i] = counts[i] + addition
            rest = rest - addition
    return np.array([bound] + counts)


def ragged(stream_key, number_of, total, most, skew):
    if number_of == 2:
        one = jax.random.randint(stream_key, (), max(1, total - most), min(most, total - 1) + 1)
        return jnp.stack([one, total - one])
    sizes = jnp.asarray(split_up(number_of, total, most, skew), jnp.int32)
    pairs = (number_of - 1) // 2
    giver, receiver = sizes[1:1 + 2 * pairs:2], sizes[2:2 + 2 * pairs:2]
    margin = jnp.minimum(giver - 1, most - receiver)
    shifted = jax.random.randint(jax.random.fold_in(stream_key, 1), (pairs,), 0, 1 << 20) % (margin + 1)
    sizes = sizes.at[1:1 + 2 * pairs:2].set(giver - shifted).at[2:2 + 2 * pairs:2].set(receiver + shifted)
    return sizes[jax.random.permutation(jax.random.fold_in(stream_key, 2), number_of)]


def gaussian(rng, shape, spread, bound, shards=(), held_as=jnp.bfloat16):
    drawn = jax.random.normal(rng, shape, jnp.float32) * spread
    if len(shards) > 0:
        drawn = level_of(rng, shape, shards, -0.22, 0.18) * drawn
    return jnp.clip(drawn, min=-bound, max=bound).astype(held_as)


def bell_draw_with(key, dims, deviation, bound, split, heavy, kind=jnp.bfloat16):
    values = deviation * jax.random.normal(key, dims, jnp.float32)
    if split:
        values = values * level_of(key, dims, split, -0.22, 0.18)
    return jnp.clip(strengthened(values, jax.random.fold_in(key, 3), *heavy), -bound, bound).astype(kind)


def setup_inputs(seed: int = 0) -> dict:
    arg_keys = jax.random.split(jax.random.key(seed), 6)
    return {
        "inputs": gaussian(arg_keys[0], (SEQS, LEN, CH), 1.0, 6.0, ((0, 16), (1, 2))),
        "cotangent": bell_draw_with(arg_keys[1], (SEQS, LEN, CH), 1.0, 6.0, ((0, 16), (1, 2)), (0, 2, 16, 2.0)),
        "segment_ids": jax.vmap(lambda own: jnp.searchsorted(jnp.cumsum(ragged(own, DOCS, LEN, DOC_MOST, 2)), jnp.arange(LEN), side="right"))(jax.random.split(arg_keys[2], SEQS)).reshape((SEQS, LEN)).astype(jnp.int32),
        "taps": gaussian(arg_keys[3], (CH, TAPS), TAPS ** -0.5, 0.5),
        "skip_gain": jnp.clip(jnp.exp(jax.random.uniform(arg_keys[4], (CH,), jnp.float32, math.log(0.5), math.log(2.0))), 0.5, 2.0),
    }


def one_sequence(carry, item):
    taps_sum, skip_sum, taps32, skip32 = carry
    inputs_seq, grads_seq, ids = item
    u32 = inputs_seq.astype(jnp.float32)
    g32 = grads_seq.astype(jnp.float32)
    reach = TAPS - 1
    length = u32.shape[0]
    g_pad = jnp.concatenate([g32, jnp.zeros((reach, CH), jnp.float32)], axis=0)
    u_pad = jnp.concatenate([jnp.zeros((reach, CH), jnp.float32), u32], axis=0)
    ids_after = jnp.concatenate([ids, jnp.full((reach,), -1, jnp.int32)])
    ids_before = jnp.concatenate([jnp.full((reach,), -1, jnp.int32), ids])

    def one_tap(acc, tap_item):
        index, column = tap_item
        g_part = lax.dynamic_slice_in_dim(g_pad, index, length, 0)
        keep_after = (lax.dynamic_slice_in_dim(ids_after, index, length, 0) == ids).astype(jnp.float32)
        acc = acc + column[None, :] * g_part * keep_after[:, None]
        u_part = lax.dynamic_slice_in_dim(u_pad, (reach - index).astype(jnp.int32), length, 0)
        keep_before = (lax.dynamic_slice_in_dim(ids_before, (reach - index).astype(jnp.int32), length, 0) == ids).astype(jnp.float32)
        column_grad = jnp.sum(g32 * u_part * keep_before[:, None], axis=0)
        return acc, column_grad

    start = jnp.zeros((length, CH), jnp.float32)
    acc, columns = lax.scan(one_tap, start, (jnp.arange(TAPS, dtype=jnp.int32), taps32.T))
    grad_in = (acc + skip32[None, :] * g32).astype(jnp.bfloat16)
    taps_sum = taps_sum + columns.T
    skip_sum = skip_sum + jnp.sum(g32 * u32, axis=0)
    return (taps_sum, skip_sum, taps32, skip32), grad_in


def reference(inputs, cotangent, segment_ids, taps, skip_gain):
    taps32 = taps.astype(jnp.float32)
    skip32 = skip_gain.astype(jnp.float32)
    init = (jnp.zeros((CH, TAPS), jnp.float32), jnp.zeros((CH,), jnp.float32), taps32, skip32)
    final, input_grad = lax.scan(one_sequence, init, (inputs, cotangent, segment_ids.astype(jnp.int32)))
    taps_grad = final[0] / SEQS
    skip_grad = final[1] / SEQS
    return input_grad, taps_grad, skip_grad
```

```python
import functools
import jax
import jax.numpy as jnp
from jax import lax
from jax.experimental import pallas as pl
from jax.experimental.pallas import tpu as pltpu
from jax.sharding import PartitionSpec as P

LANES = 128
STEP = 8
GROUP = 4
SPAN = STEP * GROUP
DOCS = 4


def up(value, unit):
    return -(-value // unit) * unit


def documents(ids_ref, info_ref):
    ids = ids_ref[...]
    begin = jnp.int32(0)
    place = jnp.int32(0)
    for doc in range(DOCS):
        count = jnp.sum(jnp.where(ids == doc, 1.0, 0.0)).astype(jnp.int32)
        spans = (count + (SPAN - 1)) // SPAN
        info_ref[doc] = begin
        info_ref[DOCS + doc] = count
        info_ref[2 * DOCS + doc] = spans
        info_ref[3 * DOCS + doc] = place
        begin = begin + count
        place = place + (spans + 1) * SPAN


def widen(refs, shards, rows, full_ref):
    for ref, shard in zip(refs, shards):
        at = pl.multiple_of(shard * rows, STEP)
        full_ref[pl.ds(at, rows), :] = ref[...].reshape(rows, LANES).astype(jnp.float32)


def separate(info_ref, g_ref, docs_ref):
    sublane = lax.broadcasted_iota(jnp.int32, (STEP, LANES), 0)
    for doc in range(DOCS):
        begin = info_ref[doc]
        count = info_ref[DOCS + doc]
        spans = info_ref[2 * DOCS + doc]
        place = info_ref[3 * DOCS + doc]

        def move(span, _):
            for i in range(GROUP):
                row = span * SPAN + i * STEP
                tile = g_ref[pl.ds(begin + row, STEP), :]
                tile = jnp.where(sublane < count - row, tile, 0.0)
                docs_ref[pl.ds(pl.multiple_of(place + row, STEP), STEP), :] = tile
            return 0

        lax.fori_loop(0, spans, move, 0)
        docs_ref[pl.ds(pl.multiple_of(place + spans * SPAN, STEP), SPAN), :] = jnp.zeros(
            (SPAN, LANES), jnp.float32
        )


def sources(me, count):
    return [lax.rem(me - k + count, count) for k in range(count)]


def filter_kernel(shards, rows, scale, me_ref, *refs):
    u_refs = refs[:shards]
    g_refs = refs[shards : 2 * shards]
    ids_ref, out_ref, info_ref, u_full, g_full, g_docs, parts = refs[2 * shards :]
    length = shards * rows
    kernel = out_ref.shape[1]

    @pl.when(pl.program_id(0) == 0)
    def _():
        documents(ids_ref, info_ref)
        u_full[length:, :] = jnp.zeros((u_full.shape[0] - length, LANES), jnp.float32)

    order = sources(me_ref[0], shards)
    widen(u_refs, order, rows, u_full)
    widen(g_refs, order, rows, g_full)
    separate(info_ref, g_full, g_docs)

    def one_part(part, _):
        sums = [jnp.zeros((STEP, LANES), jnp.float32) for _ in range(SPAN)]

        def pairs(doc, whole, span, sums):
            sums = list(sums)
            at = info_ref[doc] + span * SPAN
            base = pl.multiple_of(info_ref[3 * DOCS + doc] + (span + part) * SPAN, SPAN)
            u = [u_full[pl.ds(at + i * STEP, STEP), :] for i in range(GROUP)]
            for q in range(STEP):
                tiles = 2 * GROUP - 1 if whole else GROUP
                g = [g_docs[pl.ds(base + m * STEP + q, STEP), :] for m in range(tiles)]
                for p in range(GROUP):
                    total = None
                    for i in range(GROUP if whole else GROUP - p):
                        term = u[i] * g[i + p]
                        total = term if total is None else total + term
                    sums[p * STEP + q] = sums[p * STEP + q] + total
            return tuple(sums)

        for doc in range(DOCS):
            last = info_ref[2 * DOCS + doc] - 1 - part
            sums = lax.fori_loop(0, jnp.maximum(last, 0), functools.partial(pairs, doc, True), tuple(sums))
            edge = jnp.maximum(last, 0)
            sums = lax.fori_loop(
                edge, jnp.where(last >= 0, edge + 1, edge), functools.partial(pairs, doc, False), tuple(sums)
            )
        for k in range(SPAN):
            at = pl.multiple_of((part * SPAN + k) * STEP, STEP)
            parts[pl.ds(at, STEP), :] = sums[k]
        return 0

    lax.fori_loop(0, kernel // SPAN, one_part, 0)
    columns = []
    for block in range(kernel // STEP):
        first = block * STEP * STEP
        total = parts[pl.ds(first, STEP, stride=STEP), :]
        for r in range(1, STEP):
            total = total + parts[pl.ds(first + r, STEP, stride=STEP), :]
        columns.append(total)
    out_ref[...] = jnp.concatenate(columns, axis=0).T * scale


def grad_kernel(shards, rows, me_ref, *refs):
    g_refs = refs[:shards]
    ids_ref, taps_ref, skip_ref = refs[shards : shards + 3]
    out_refs = refs[shards + 3 : 2 * shards + 3]
    info_ref, g_full, g_docs, taps_full, total_ref = refs[2 * shards + 3 :]
    length = shards * rows
    kernel = taps_ref.shape[1]

    @pl.when(pl.program_id(0) == 0)
    def _():
        documents(ids_ref, info_ref)

    order = sources(me_ref[0], shards)
    widen(g_refs, order, rows, g_full)
    separate(info_ref, g_full, g_docs)
    taps_full[...] = taps_ref[...].astype(jnp.float32).T
    total_ref[:length, :] = g_full[:length, :] * skip_ref[...]

    def one_part(part, _):
        taps = [taps_full[pl.ds(part * SPAN + k, STEP, stride=0), :] for k in range(SPAN)]

        def pairs(doc, whole, span, _):
            at = info_ref[doc] + span * SPAN
            base = pl.multiple_of(info_ref[3 * DOCS + doc] + (span + part) * SPAN, SPAN)
            total = [total_ref[pl.ds(at + i * STEP, STEP), :] for i in range(GROUP)]
            for q in range(STEP):
                tiles = 2 * GROUP - 1 if whole else GROUP
                g = [g_docs[pl.ds(base + m * STEP + q, STEP), :] for m in range(tiles)]
                for p in range(GROUP):
                    for i in range(GROUP if whole else GROUP - p):
                        total[i] = total[i] + taps[p * STEP + q] * g[i + p]
            for i in range(GROUP):
                total_ref[pl.ds(at + i * STEP, STEP), :] = total[i]
            return 0

        for doc in range(DOCS):
            last = info_ref[2 * DOCS + doc] - 1 - part
            edge = jnp.maximum(last, 0)
            lax.fori_loop(0, edge, functools.partial(pairs, doc, True), 0)
            lax.fori_loop(edge, jnp.where(last >= 0, edge + 1, edge), functools.partial(pairs, doc, False), 0)
        return 0

    lax.fori_loop(0, kernel // SPAN, one_part, 0)
    for out_ref, shard in zip(out_refs, order):
        at = pl.multiple_of(shard * rows, STEP)
        out_ref[...] = total_ref[pl.ds(at, rows), :].astype(out_ref.dtype).reshape(out_ref.shape)


def sizes(shards, rows):
    length = shards * rows
    docs_rows = up(length, SPAN) + 2 * DOCS * SPAN
    return length + SPAN, docs_rows


def filter_part(me, u_list, g_list, ids, kernel, scale, width, first, count):
    shards = len(u_list)
    rows = u_list[0].shape[1]
    blocks = width // LANES
    tall, docs_rows = sizes(shards, rows)
    data = pl.BlockSpec((1, rows, LANES), lambda c, me_ref: (0, 0, me_ref[0] * blocks + first + c))
    pairs = 5 * rows * shards * kernel * count * LANES // 16
    return pl.pallas_call(
        functools.partial(filter_kernel, shards, rows, scale),
        out_shape=jax.ShapeDtypeStruct((count * LANES, kernel), jnp.float32),
        grid_spec=pltpu.PrefetchScalarGridSpec(
            num_scalar_prefetch=1,
            grid=(count,),
            in_specs=[data] * (2 * shards) + [pl.BlockSpec(ids.shape, lambda c, me_ref: (0, 0))],
            out_specs=pl.BlockSpec((LANES, kernel), lambda c, me_ref: (c, 0)),
            scratch_shapes=[
                pltpu.SMEM((4 * DOCS,), jnp.int32),
                pltpu.VMEM((tall, LANES), jnp.float32),
                pltpu.VMEM((tall, LANES), jnp.float32),
                pltpu.VMEM((docs_rows, LANES), jnp.float32),
                pltpu.VMEM((kernel * STEP, LANES), jnp.float32),
            ],
        ),
        cost_estimate=pl.CostEstimate(
            flops=2 * pairs, bytes_accessed=count * LANES * (4 * rows * shards + 4 * kernel), transcendentals=0
        ),
    )(me, *u_list, *g_list, ids)


def grad_part(me, g_list, ids, taps, skip_gain, width):
    shards = len(g_list)
    rows = g_list[0].shape[1]
    kernel = taps.shape[1]
    blocks = width // LANES
    tall, docs_rows = sizes(shards, rows)
    data = pl.BlockSpec((1, rows, LANES), lambda c, me_ref: (0, 0, me_ref[0] * blocks + c))
    pairs = 5 * rows * shards * kernel * width // 16
    return pl.pallas_call(
        functools.partial(grad_kernel, shards, rows),
        out_shape=[jax.ShapeDtypeStruct((1, rows, width), jnp.bfloat16)] * shards,
        grid_spec=pltpu.PrefetchScalarGridSpec(
            num_scalar_prefetch=1,
            grid=(blocks,),
            in_specs=[data] * shards
            + [
                pl.BlockSpec(ids.shape, lambda c, me_ref: (0, 0)),
                pl.BlockSpec((LANES, kernel), lambda c, me_ref: (me_ref[0] * blocks + c, 0)),
                pl.BlockSpec((1, LANES), lambda c, me_ref: (0, me_ref[0] * blocks + c)),
            ],
            out_specs=[pl.BlockSpec((1, rows, LANES), lambda c, me_ref: (0, 0, c))] * shards,
            scratch_shapes=[
                pltpu.SMEM((4 * DOCS,), jnp.int32),
                pltpu.VMEM((tall, LANES), jnp.float32),
                pltpu.VMEM((docs_rows, LANES), jnp.float32),
                pltpu.VMEM((kernel, LANES), jnp.float32),
                pltpu.VMEM((tall, LANES), jnp.float32),
            ],
        ),
        cost_estimate=pl.CostEstimate(
            flops=2 * pairs, bytes_accessed=width * (4 * rows * shards + 2 * kernel), transcendentals=0
        ),
    )(me, *g_list, ids, taps, skip_gain.reshape(1, -1))


CHUNKS = 2


def shifted(array, axis, count, step):
    return lax.ppermute(array, axis, [(i, (i + step) % count) for i in range(count)])


def reduced(part, axis, count):
    rows = up(part.shape[0], count)
    part = jnp.pad(part, ((0, rows - part.shape[0]), (0, 0)))
    pieces = lax.all_to_all(part.reshape(count, rows // count, -1), axis, 0, 0, tiled=True)
    return jnp.sum(pieces, axis=0)


def gathered(piece, axis, count, rows):
    copies = jnp.broadcast_to(piece[None], (count,) + piece.shape)
    return lax.all_to_all(copies, axis, 0, 0, tiled=True).reshape(-1, piece.shape[1])[:rows]


def shards(inputs, cotangent, segment_ids, taps, skip_gain):
    count = lax.axis_size("ctx")
    groups = lax.axis_size("dp")
    me = lax.axis_index("ctx").astype(jnp.int32)[None]
    width = inputs.shape[2] // count
    scale = 1.0 / (inputs.shape[0] * groups)
    u_list = [inputs] + [shifted(inputs, "ctx", count, k) for k in range(1, count)]
    g_list = [cotangent] + [shifted(cotangent, "ctx", count, k) for k in range(1, count)]
    blocks = width // LANES
    each = blocks // CHUNKS
    kernel = taps.shape[1]
    shares = []
    for chunk in range(CHUNKS):
        part = filter_part(me, u_list, g_list, segment_ids, kernel, scale, width, chunk * each, each)
        shares.append(reduced(part, "dp", groups))
    parts = grad_part(me, g_list, segment_ids, taps, skip_gain, width)
    whole = [gathered(share, "dp", groups, each * LANES) for share in shares]
    taps_grad = jnp.concatenate(whole, axis=0)
    input_grad = jnp.zeros(inputs.shape, jnp.bfloat16)
    for k in range(count):
        got = parts[k] if k == 0 else shifted(parts[k], "ctx", count, -k)
        owner = lax.rem(me[0] + k, count) if k else me[0]
        input_grad = lax.dynamic_update_slice(input_grad, got, (0, 0, owner * width))
    return input_grad, taps_grad, taps_grad[:, 0]


def solution(mesh):
    return jax.shard_map(
        shards,
        mesh=mesh,
        in_specs=(P("dp", "ctx", None), P("dp", "ctx", None), P("dp", None), P(), P()),
        out_specs=(P("dp", "ctx", None), P("ctx", None), P("ctx")),
        check_vma=False,
    )
```

```python
import functools
import math
import jax
import jax.numpy as jnp
import numpy as np
from jax import lax
from jax.experimental import pallas as pl
from jax.experimental.pallas import tpu as pltpu
from jax.sharding import PartitionSpec as P

LANES = 128
STEP = 8
TILES = 2
BLOCK = LANES * TILES
DOCS = 4


def up(value, unit):
    return -(-value // unit) * unit


def halves(table):
    high = np.asarray(table, np.float32).astype(jnp.bfloat16)
    low = (np.asarray(table, np.float64) - high.astype(np.float64)).astype(np.float32).astype(jnp.bfloat16)
    return high, low


def tables(most, kernel):
    period = most + kernel
    waves = period // 2
    angle = np.pi * np.outer(2 * np.arange(waves) + 1, np.arange(most)) / period
    ahead = halves(np.concatenate([np.cos(angle), -np.sin(angle)], axis=0))
    back = halves(np.concatenate([np.cos(angle), -np.sin(angle)], axis=0).T / waves)
    ahead = np.concatenate(ahead, axis=1)
    back = np.concatenate([back[0], back[0], back[1]], axis=1)
    return ahead, back


def spectrum(table, value):
    return jnp.dot(table, jnp.concatenate([value, value], axis=0), preferred_element_type=jnp.float32)


def against(left, right):
    waves = left.shape[0] // 2
    lr, li = left[:waves], left[waves:]
    rr, ri = right[:waves], right[waves:]
    return lr * rr + li * ri, li * rr - lr * ri


def inverse(table, real, imag):
    value = jnp.concatenate([real, imag], axis=0)
    high = value.astype(jnp.bfloat16)
    low = (value - high.astype(jnp.float32)).astype(jnp.bfloat16)
    return jnp.dot(table, jnp.concatenate([high, low, high], axis=0), preferred_element_type=jnp.float32)


def documents(ids_ref, info_ref):
    ids = ids_ref[...]
    begin = jnp.int32(0)
    for doc in range(DOCS):
        count = jnp.sum(jnp.where(ids == doc, 1.0, 0.0)).astype(jnp.int32)
        info_ref[doc] = begin
        info_ref[DOCS + doc] = count
        begin = begin + count


def widen(refs, shards, rows, full_ref):
    for ref, shard in zip(refs, shards):
        at = pl.multiple_of(shard * rows, STEP)
        for tile in range(TILES):
            block = ref[0, :, tile * LANES : (tile + 1) * LANES]
            full_ref[tile, pl.ds(at, rows), :] = block.astype(jnp.float32)


def window(full_ref, begin, most, count=None):
    tiles = []
    for tile in range(TILES):
        column = [full_ref[tile, pl.ds(begin + i, STEP), :] for i in range(0, most, STEP)]
        tiles.append(jnp.concatenate(column, axis=0))
    value = jnp.concatenate(tiles, axis=1)
    if count is not None:
        value = jnp.where(lax.broadcasted_iota(jnp.int32, value.shape, 0) < count, value, 0.0)
    return value.astype(jnp.bfloat16)


def sources(me, count):
    return [lax.rem(me - k + count, count) for k in range(count)]


def filter_kernel(shards, rows, most, scale, me_ref, *refs):
    u_refs = refs[:shards]
    g_refs = refs[shards : 2 * shards]
    ids_ref, ahead_ref, back_ref, out_ref, info_ref, u_full, g_full = refs[2 * shards :]
    length = shards * rows
    kernel = out_ref.shape[1]

    @pl.when(pl.program_id(0) == 0)
    def _():
        documents(ids_ref, info_ref)
        u_full[:, length:, :] = jnp.zeros((TILES, most, LANES), jnp.float32)

    order = sources(me_ref[0], shards)
    widen(u_refs, order, rows, u_full)
    widen(g_refs, order, rows, g_full)
    ahead = ahead_ref[...]
    real, imag = 0.0, 0.0
    for doc in range(DOCS):
        begin = info_ref[doc]
        g_wave = spectrum(ahead, window(g_full, begin, most, info_ref[DOCS + doc]))
        u_wave = spectrum(ahead, window(u_full, begin, most))
        add_real, add_imag = against(g_wave, u_wave)
        real, imag = real + add_real, imag + add_imag
    taps = inverse(back_ref[:kernel, :], real, imag) * scale
    for tile in range(TILES):
        at = tile * LANES
        out_ref[at : at + LANES, :] = taps[:, at : at + LANES].T


def grad_kernel(shards, rows, most, me_ref, *refs):
    g_refs = refs[:shards]
    ids_ref, ahead_ref, head_ref, back_ref, taps_ref, skip_ref = refs[shards : shards + 6]
    out_refs = refs[shards + 6 : 2 * shards + 6]
    info_ref, g_full, total_ref = refs[2 * shards + 6 :]

    @pl.when(pl.program_id(0) == 0)
    def _():
        documents(ids_ref, info_ref)

    order = sources(me_ref[0], shards)
    widen(g_refs, order, rows, g_full)
    ahead = ahead_ref[...]
    taps = taps_ref[...]
    h_wave = lax.dot_general(
        head_ref[...],
        jnp.concatenate([taps, taps], axis=1),
        (((1,), (1,)), ((), ())),
        preferred_element_type=jnp.float32,
    )
    for doc in range(DOCS):
        begin = info_ref[doc]
        g_wave = spectrum(ahead, window(g_full, begin, most, info_ref[DOCS + doc]))
        total = inverse(back_ref[...], *against(g_wave, h_wave))
        for tile in range(TILES):
            for i in range(0, most, STEP):
                total_ref[tile, pl.ds(begin + i, STEP), :] = total[i : i + STEP, tile * LANES : (tile + 1) * LANES]
    for out_ref, shard in zip(out_refs, order):
        at = pl.multiple_of(shard * rows, STEP)
        for tile in range(TILES):
            lanes = slice(tile * LANES, (tile + 1) * LANES)
            skipped = g_full[tile, pl.ds(at, rows), :] * skip_ref[:, lanes]
            out_ref[0, :, lanes] = (total_ref[tile, pl.ds(at, rows), :] + skipped).astype(out_ref.dtype)


def filter_part(me, u_list, g_list, ids, kernel, scale, width, first, count):
    shards = len(u_list)
    rows = u_list[0].shape[1]
    length = shards * rows
    most = length // 2
    blocks = width // BLOCK
    ahead, back = tables(most, kernel)
    data = pl.BlockSpec((1, rows, BLOCK), lambda c, me_ref: (0, 0, me_ref[0] * blocks + first + c))
    fixed = lambda array: pl.BlockSpec(array.shape, lambda c, me_ref: (0, 0))
    return pl.pallas_call(
        functools.partial(filter_kernel, shards, rows, most, scale),
        out_shape=jax.ShapeDtypeStruct((count * BLOCK, kernel), jnp.float32),
        grid_spec=pltpu.PrefetchScalarGridSpec(
            num_scalar_prefetch=1,
            grid=(count,),
            in_specs=[data] * (2 * shards) + [fixed(ids), fixed(ahead), fixed(back)],
            out_specs=pl.BlockSpec((BLOCK, kernel), lambda c, me_ref: (c, 0)),
            scratch_shapes=[
                pltpu.SMEM((2 * DOCS,), jnp.int32),
                pltpu.VMEM((TILES, length + most, LANES), jnp.float32),
                pltpu.VMEM((TILES, length + most, LANES), jnp.float32),
            ],
        ),
        cost_estimate=pl.CostEstimate(
            flops=2 * count * BLOCK * (2 * DOCS * ahead.size + kernel * back.shape[1]),
            bytes_accessed=count * BLOCK * (4 * length + 4 * kernel),
            transcendentals=0,
        ),
    )(me, *u_list, *g_list, ids, jnp.asarray(ahead), jnp.asarray(back))


def grad_part(me, g_list, ids, taps, skip_gain, width, first, count):
    shards = len(g_list)
    rows = g_list[0].shape[1]
    kernel = taps.shape[1]
    length = shards * rows
    most = length // 2
    blocks = width // BLOCK
    ahead, back = tables(most, kernel)
    head = np.concatenate([ahead[:, :kernel], ahead[:, most : most + kernel]], axis=1)
    data = pl.BlockSpec((1, rows, BLOCK), lambda c, me_ref: (0, 0, me_ref[0] * blocks + first + c))
    fixed = lambda array: pl.BlockSpec(array.shape, lambda c, me_ref: (0, 0))
    return pl.pallas_call(
        functools.partial(grad_kernel, shards, rows, most),
        out_shape=[jax.ShapeDtypeStruct((1, rows, count * BLOCK), jnp.bfloat16)] * shards,
        grid_spec=pltpu.PrefetchScalarGridSpec(
            num_scalar_prefetch=1,
            grid=(count,),
            in_specs=[data] * shards
            + [fixed(ids), fixed(ahead), fixed(head), fixed(back)]
            + [
                pl.BlockSpec((BLOCK, kernel), lambda c, me_ref: (me_ref[0] * blocks + first + c, 0)),
                pl.BlockSpec((1, BLOCK), lambda c, me_ref: (0, me_ref[0] * blocks + first + c)),
            ],
            out_specs=[pl.BlockSpec((1, rows, BLOCK), lambda c, me_ref: (0, 0, c))] * shards,
            scratch_shapes=[
                pltpu.SMEM((2 * DOCS,), jnp.int32),
                pltpu.VMEM((TILES, length + most, LANES), jnp.float32),
                pltpu.VMEM((TILES, length + most, LANES), jnp.float32),
            ],
        ),
        cost_estimate=pl.CostEstimate(
            flops=2 * count * BLOCK * (DOCS * (ahead.size + back.size) + head.size),
            bytes_accessed=count * BLOCK * (4 * length + 2 * kernel),
            transcendentals=0,
        ),
    )(me, *g_list, ids, jnp.asarray(ahead), jnp.asarray(head), jnp.asarray(back), taps, skip_gain.reshape(1, -1))


CHUNKS = 1


def shifted(array, axis, count, step):
    return lax.ppermute(array, axis, [(i, (i + step) % count) for i in range(count)])


def reduced(part, axis, count):
    rows = up(part.shape[0], count)
    part = jnp.pad(part, ((0, rows - part.shape[0]), (0, 0)))
    pieces = lax.all_to_all(part.reshape(count, rows // count, -1), axis, 0, 0, tiled=True)
    return jnp.sum(pieces, axis=0)


def gathered(piece, axis, count, rows):
    copies = jnp.broadcast_to(piece[None], (count,) + piece.shape)
    return lax.all_to_all(copies, axis, 0, 0, tiled=True).reshape(-1, piece.shape[1])[:rows]


def shards(inputs, cotangent, segment_ids, taps, skip_gain):
    count = lax.axis_size("ctx")
    groups = lax.axis_size("dp")
    me = lax.axis_index("ctx").astype(jnp.int32)[None]
    width = inputs.shape[2] // count
    scale = 1.0 / (inputs.shape[0] * groups)
    u_list = [inputs] + [shifted(inputs, "ctx", count, k) for k in range(1, count)]
    g_list = [cotangent] + [shifted(cotangent, "ctx", count, k) for k in range(1, count)]
    blocks = width // BLOCK
    each = blocks // CHUNKS
    kernel = taps.shape[1]
    shares = []
    for chunk in range(CHUNKS):
        part = filter_part(me, u_list, g_list, segment_ids, kernel, scale, width, chunk * each, each)
        shares.append(reduced(part, "dp", groups))
    parts = grad_part(me, g_list, segment_ids, taps, skip_gain, width, 0, blocks)
    whole = [gathered(share, "dp", groups, each * BLOCK) for share in shares]
    taps_grad = jnp.concatenate(whole, axis=0)
    input_grad = jnp.zeros(inputs.shape, jnp.bfloat16)
    for k in range(count):
        got = parts[k] if k == 0 else shifted(parts[k], "ctx", count, -k)
        owner = lax.rem(me[0] + k, count) if k else me[0]
        input_grad = lax.dynamic_update_slice(input_grad, got, (0, 0, owner * width))
    return input_grad, taps_grad, taps_grad[:, 0]


def solution(mesh):
    return jax.shard_map(
        shards,
        mesh=mesh,
        in_specs=(P("dp", "ctx", None), P("dp", "ctx", None), P("dp", None), P(), P()),
        out_specs=(P("dp", "ctx", None), P("ctx", None), P("ctx")),
        check_vma=False,
    )
```

```python
import functools
import math
import jax
import jax.numpy as jnp
import numpy as np
from jax import lax
from jax.experimental import pallas as pl
from jax.experimental.pallas import tpu as pltpu
from jax.sharding import PartitionSpec as P

LANES = 128
STEP = 8
TILES = 2
BLOCK = LANES * TILES
DOCS = 4
TOP = 12.0
NOTE = STEP
TINY = 1e-30


def up(value, unit):
    return -(-value // unit) * unit


def halves(table):
    high = np.asarray(table, np.float32).astype(jnp.bfloat16)
    low = (np.asarray(table, np.float64) - high.astype(np.float64)).astype(np.float32).astype(jnp.bfloat16)
    return high, low


def tables(most, kernel):
    period = most + kernel
    waves = period // 2
    angle = np.pi * np.outer(2 * np.arange(waves) + 1, np.arange(most)) / period
    ahead = halves(np.concatenate([np.cos(angle), -np.sin(angle)], axis=0))
    back = halves(np.concatenate([np.cos(angle), -np.sin(angle)], axis=0).T / waves)
    ahead = np.concatenate(ahead, axis=1)
    back = np.concatenate([back[0], back[0], back[1]], axis=1)
    return ahead, back


def spectrum(table, value):
    return jnp.dot(table, jnp.concatenate([value, value], axis=0), preferred_element_type=jnp.float32)


def against(left, right):
    waves = left.shape[0] // 2
    lr, li = left[:waves], left[waves:]
    rr, ri = right[:waves], right[waves:]
    return lr * rr + li * ri, li * rr - lr * ri


def inverse(table, real, imag):
    value = jnp.concatenate([real, imag], axis=0)
    high = value.astype(jnp.bfloat16)
    low = (value - high.astype(jnp.float32)).astype(jnp.bfloat16)
    return jnp.dot(table, jnp.concatenate([high, low, high], axis=0), preferred_element_type=jnp.float32)


def documents(ids_ref, info_ref):
    ids = ids_ref[...]
    begin = jnp.int32(0)
    for doc in range(DOCS):
        count = jnp.sum(jnp.where(ids == doc, 1.0, 0.0)).astype(jnp.int32)
        info_ref[doc] = begin
        info_ref[DOCS + doc] = count
        begin = begin + count


def widen(refs, shards, rows, full_ref):
    for ref, shard in zip(refs, shards):
        at = pl.multiple_of(shard * rows, STEP)
        for tile in range(TILES):
            block = ref[0, :, tile * LANES : (tile + 1) * LANES]
            full_ref[tile, pl.ds(at, rows), :] = block.astype(jnp.float32)


def window(full_ref, begin, most, count=None):
    tiles = []
    for tile in range(TILES):
        column = [full_ref[tile, pl.ds(begin + i, STEP), :] for i in range(0, most, STEP)]
        tiles.append(jnp.concatenate(column, axis=0))
    value = jnp.concatenate(tiles, axis=1)
    if count is not None:
        value = jnp.where(lax.broadcasted_iota(jnp.int32, value.shape, 0) < count, value, 0.0)
    return value.astype(jnp.bfloat16)


def sources(me, count):
    return [lax.rem(me - k + count, count) for k in range(count)]


def power(exponent):
    return jnp.exp(exponent * math.log(2.0))


def exponent_of(peak):
    return jnp.ceil(jnp.log(jnp.maximum(peak, TINY)) * (1.0 / math.log(2.0)))


def filter_kernel(shards, rows, most, scale, packed, me_ref, *refs):
    u_refs = refs[:shards]
    g_refs = refs[shards : 2 * shards]
    ids_ref, ahead_ref, back_ref, out_ref, info_ref, u_full, g_full = refs[2 * shards :]
    length = shards * rows
    kernel = LANES

    @pl.when(pl.program_id(0) == 0)
    def _():
        documents(ids_ref, info_ref)
        u_full[:, length:, :] = jnp.zeros((TILES, most, LANES), jnp.float32)

    order = sources(me_ref[0], shards)
    widen(u_refs, order, rows, u_full)
    widen(g_refs, order, rows, g_full)
    ahead = ahead_ref[...]
    real, imag = 0.0, 0.0
    for doc in range(DOCS):
        begin = info_ref[doc]
        g_wave = spectrum(ahead, window(g_full, begin, most, info_ref[DOCS + doc]))
        u_wave = spectrum(ahead, window(u_full, begin, most))
        add_real, add_imag = against(g_wave, u_wave)
        real, imag = real + add_real, imag + add_imag
    taps = inverse(back_ref[:kernel, :], real, imag) * scale
    if packed:
        exponent = exponent_of(jnp.max(jnp.abs(taps), axis=0, keepdims=True))
        taps = taps * power(TOP - exponent)
    for tile in range(TILES):
        at = tile * LANES
        if packed:
            out_ref[tile, :kernel, :] = taps[:, at : at + LANES]
            out_ref[tile, kernel:, :] = jnp.broadcast_to(exponent[:, at : at + LANES], (NOTE, LANES))
        else:
            out_ref[at : at + LANES, :] = taps[:, at : at + LANES].T


def total_kernel(pieces_ref, out_ref):
    kernel = pieces_ref.shape[1] - NOTE
    total = jnp.zeros((kernel, LANES), jnp.float32)
    for k in range(pieces_ref.shape[0]):
        total = total + pieces_ref[k, :kernel, :] * power(pieces_ref[k, kernel : kernel + 1, :] - TOP)
    peak = jnp.max(jnp.max(jnp.abs(total), axis=0, keepdims=True), axis=1, keepdims=True)
    exponent = exponent_of(peak)
    total = total * power(TOP - exponent)
    out_ref[:LANES, :] = total.T
    row = lax.broadcasted_iota(jnp.int32, (NOTE, LANES), 0)
    out_ref[LANES:, :] = jnp.where(row == 0, exponent, total[:1, :])


def total_part(pieces):
    return pl.pallas_call(
        total_kernel, out_shape=jax.ShapeDtypeStruct((LANES + NOTE, pieces.shape[1] - NOTE), jnp.float32)
    )(pieces)


def grad_kernel(shards, rows, most, me_ref, *refs):
    g_refs = refs[:shards]
    ids_ref, ahead_ref, head_ref, back_ref, taps_ref, skip_ref = refs[shards : shards + 6]
    out_refs = refs[shards + 6 : 2 * shards + 6]
    info_ref, g_full, total_ref = refs[2 * shards + 6 :]

    @pl.when(pl.program_id(0) == 0)
    def _():
        documents(ids_ref, info_ref)

    order = sources(me_ref[0], shards)
    widen(g_refs, order, rows, g_full)
    ahead = ahead_ref[...]
    taps = taps_ref[...]
    h_wave = lax.dot_general(
        head_ref[...],
        jnp.concatenate([taps, taps], axis=1),
        (((1,), (1,)), ((), ())),
        preferred_element_type=jnp.float32,
    )
    for doc in range(DOCS):
        begin = info_ref[doc]
        g_wave = spectrum(ahead, window(g_full, begin, most, info_ref[DOCS + doc]))
        total = inverse(back_ref[...], *against(g_wave, h_wave))
        for tile in range(TILES):
            for i in range(0, most, STEP):
                total_ref[tile, pl.ds(begin + i, STEP), :] = total[i : i + STEP, tile * LANES : (tile + 1) * LANES]
    for out_ref, shard in zip(out_refs, order):
        at = pl.multiple_of(shard * rows, STEP)
        for tile in range(TILES):
            lanes = slice(tile * LANES, (tile + 1) * LANES)
            skipped = g_full[tile, pl.ds(at, rows), :] * skip_ref[:, lanes]
            out_ref[0, :, lanes] = (total_ref[tile, pl.ds(at, rows), :] + skipped).astype(out_ref.dtype)


def filter_part(me, u_list, g_list, ids, kernel, scale, width, packed):
    shards = len(u_list)
    rows = u_list[0].shape[1]
    length = shards * rows
    most = length // 2
    blocks = width // BLOCK
    ahead, back = tables(most, kernel)
    data = pl.BlockSpec((1, rows, BLOCK), lambda c, me_ref: (0, 0, me_ref[0] * blocks + c))
    fixed = lambda array: pl.BlockSpec(array.shape, lambda c, me_ref: (0, 0))
    if packed:
        shape = (width // LANES, kernel + NOTE, LANES)
        out_spec = pl.BlockSpec((TILES,) + shape[1:], lambda c, me_ref: (c, 0, 0))
    else:
        shape = (width, kernel)
        out_spec = pl.BlockSpec((BLOCK, kernel), lambda c, me_ref: (c, 0))
    return pl.pallas_call(
        functools.partial(filter_kernel, shards, rows, most, scale, packed),
        out_shape=jax.ShapeDtypeStruct(shape, jnp.float32),
        grid_spec=pltpu.PrefetchScalarGridSpec(
            num_scalar_prefetch=1,
            grid=(blocks,),
            in_specs=[data] * (2 * shards) + [fixed(ids), fixed(ahead), fixed(back)],
            out_specs=out_spec,
            scratch_shapes=[
                pltpu.SMEM((2 * DOCS,), jnp.int32),
                pltpu.VMEM((TILES, length + most, LANES), jnp.float32),
                pltpu.VMEM((TILES, length + most, LANES), jnp.float32),
            ],
        ),
        cost_estimate=pl.CostEstimate(
            flops=2 * width * (2 * DOCS * ahead.size + kernel * back.shape[1]),
            bytes_accessed=width * (4 * length + 4 * kernel),
            transcendentals=0,
        ),
    )(me, *u_list, *g_list, ids, jnp.asarray(ahead), jnp.asarray(back))


def grad_part(me, g_list, ids, taps, skip_gain, width):
    shards = len(g_list)
    rows = g_list[0].shape[1]
    kernel = taps.shape[1]
    length = shards * rows
    most = length // 2
    blocks = width // BLOCK
    ahead, back = tables(most, kernel)
    head = np.concatenate([ahead[:, :kernel], ahead[:, most : most + kernel]], axis=1)
    data = pl.BlockSpec((1, rows, BLOCK), lambda c, me_ref: (0, 0, me_ref[0] * blocks + c))
    fixed = lambda array: pl.BlockSpec(array.shape, lambda c, me_ref: (0, 0))
    return pl.pallas_call(
        functools.partial(grad_kernel, shards, rows, most),
        out_shape=[jax.ShapeDtypeStruct((1, rows, width), jnp.bfloat16)] * shards,
        grid_spec=pltpu.PrefetchScalarGridSpec(
            num_scalar_prefetch=1,
            grid=(blocks,),
            in_specs=[data] * shards
            + [fixed(ids), fixed(ahead), fixed(head), fixed(back)]
            + [
                pl.BlockSpec((BLOCK, kernel), lambda c, me_ref: (me_ref[0] * blocks + c, 0)),
                pl.BlockSpec((1, BLOCK), lambda c, me_ref: (0, me_ref[0] * blocks + c)),
            ],
            out_specs=[pl.BlockSpec((1, rows, BLOCK), lambda c, me_ref: (0, 0, c))] * shards,
            scratch_shapes=[
                pltpu.SMEM((2 * DOCS,), jnp.int32),
                pltpu.VMEM((TILES, length + most, LANES), jnp.float32),
                pltpu.VMEM((TILES, length + most, LANES), jnp.float32),
            ],
        ),
        cost_estimate=pl.CostEstimate(
            flops=2 * width * (DOCS * (ahead.size + back.size) + head.size),
            bytes_accessed=width * (4 * length + 2 * kernel),
            transcendentals=0,
        ),
    )(me, *g_list, ids, jnp.asarray(ahead), jnp.asarray(head), jnp.asarray(back), taps, skip_gain.reshape(1, -1))


def shifted(array, axis, count, step):
    return lax.ppermute(array, axis, [(i, (i + step) % count) for i in range(count)])


def exchanged(pieces, axis):
    return lax.all_to_all(pieces, axis, 0, 0, tiled=True)


def packed_sum(parts, axis, count):
    pieces = exchanged(parts.astype(jnp.float16), axis).astype(jnp.float32)
    piece = total_part(pieces).astype(jnp.float16)
    pieces = exchanged(jnp.broadcast_to(piece[None], (count,) + piece.shape), axis)
    pieces = pieces.astype(jnp.float32)
    weight = power(pieces[:, LANES, :1] - TOP)
    whole = pieces[:, :LANES, :] * weight[:, :, None]
    skip = pieces[:, LANES + 1, :] * weight
    return whole.reshape(count * LANES, -1), skip.reshape(-1)


def plain_sum(parts, axis, count):
    rows = up(parts.shape[0], count)
    padded = jnp.pad(parts, ((0, rows - parts.shape[0]), (0, 0)))
    piece = jnp.sum(exchanged(padded.reshape(count, rows // count, -1), axis), axis=0)
    whole = exchanged(jnp.broadcast_to(piece[None], (count,) + piece.shape), axis)
    whole = whole.reshape(rows, -1)[: parts.shape[0]]
    return whole, whole[:, 0]


def shards(inputs, cotangent, segment_ids, taps, skip_gain):
    count = lax.axis_size("ctx")
    groups = lax.axis_size("dp")
    me = lax.axis_index("ctx").astype(jnp.int32)[None]
    width = inputs.shape[2] // count
    kernel = taps.shape[1]
    scale = 1.0 / (inputs.shape[0] * groups)
    packed = width == groups * LANES and kernel == LANES
    u_list = [inputs] + [shifted(inputs, "ctx", count, k) for k in range(1, count)]
    g_list = [cotangent] + [shifted(cotangent, "ctx", count, k) for k in range(1, count)]
    parts = filter_part(me, u_list, g_list, segment_ids, kernel, scale, width, packed)
    taps_grad, skip_grad = (packed_sum if packed else plain_sum)(parts, "dp", groups)
    grads = grad_part(me, g_list, segment_ids, taps, skip_gain, width)
    input_grad = jnp.zeros(inputs.shape, jnp.bfloat16)
    for k in range(count):
        got = grads[k] if k == 0 else shifted(grads[k], "ctx", count, -k)
        owner = lax.rem(me[0] + k, count)
        input_grad = lax.dynamic_update_slice(input_grad, got, (0, 0, owner * width))
    return input_grad, taps_grad, skip_grad


def solution(mesh):
    return jax.shard_map(
        shards,
        mesh=mesh,
        in_specs=(P("dp", "ctx", None), P("dp", "ctx", None), P("dp", None), P(), P()),
        out_specs=(P("dp", "ctx", None), P("ctx", None), P("ctx")),
        check_vma=False,
    )
```

```python
import functools
import math
import jax
import jax.numpy as jnp
import numpy as np
from jax import lax
from jax.experimental import pallas as pl
from jax.experimental.pallas import tpu as pltpu
from jax.sharding import PartitionSpec as P

LANES = 128
STEP = 8
TILES = 2
SUBS = 2
BLOCK = LANES * TILES
DOCS = 4
TOP = 12.0
NOTE = STEP
TINY = 1e-30


def up(value, unit):
    return -(-value // unit) * unit


def halves(table):
    high = np.asarray(table, np.float32).astype(jnp.bfloat16)
    low = (np.asarray(table, np.float64) - high.astype(np.float64)).astype(np.float32).astype(jnp.bfloat16)
    return high, low


def tables(most, kernel):
    period = most + kernel
    waves = period // 2
    angle = np.pi * np.outer(2 * np.arange(waves) + 1, np.arange(most)) / period
    pair = np.stack([np.cos(angle).reshape(-1, STEP, most), -np.sin(angle).reshape(-1, STEP, most)], axis=1)
    pair = pair.reshape(period, most)
    ahead = np.concatenate(halves(pair), axis=1)
    back = halves(pair.T / waves)
    back = np.concatenate([back[0], back[0], back[1]], axis=1)
    return ahead, back


def spectrum(table, value):
    return jnp.dot(table, jnp.concatenate([value, value], axis=0), preferred_element_type=jnp.float32)


def against(left, right):
    product = []
    for at in range(0, left.shape[0], 2 * STEP):
        lr, li = left[at : at + STEP], left[at + STEP : at + 2 * STEP]
        rr, ri = right[at : at + STEP], right[at + STEP : at + 2 * STEP]
        product += [lr * rr + li * ri, li * rr - lr * ri]
    return product


def inverse(table, product):
    high, low = [], []
    for at in range(0, len(product), 2):
        value = jnp.concatenate(product[at : at + 2], axis=0)
        high.append(value.astype(jnp.bfloat16))
        low.append((value - high[-1].astype(jnp.float32)).astype(jnp.bfloat16))
    return jnp.dot(table, jnp.concatenate(high + low + high, axis=0), preferred_element_type=jnp.float32)


def documents(ids_ref, info_ref):
    ids = ids_ref[...]
    begin = jnp.int32(0)
    for doc in range(DOCS):
        count = jnp.sum(jnp.where(ids == doc, 1.0, 0.0)).astype(jnp.int32)
        info_ref[doc] = begin
        info_ref[DOCS + doc] = count
        begin = begin + count


def widen(refs, shards, rows, full_ref, sub, base):
    for k, (ref, shard) in enumerate(zip(refs, shards)):
        at = pl.multiple_of(shard * rows, STEP)
        for tile in range(TILES):
            first = sub * BLOCK + tile * LANES
            if k:
                first = pl.multiple_of(base + first, LANES)
            block = ref[0, :, pl.ds(first, LANES)]
            full_ref[tile, pl.ds(at, rows), :] = block.astype(jnp.float32)


def window(full_ref, begin, most, count=None):
    tiles = []
    for tile in range(TILES):
        column = [full_ref[tile, pl.ds(begin + i, STEP), :] for i in range(0, most, STEP)]
        tiles.append(jnp.concatenate(column, axis=0))
    value = jnp.concatenate(tiles, axis=1)
    if count is not None:
        value = jnp.where(lax.broadcasted_iota(jnp.int32, value.shape, 0) < count, value, 0.0)
    return value.astype(jnp.bfloat16)


def sources(me, count):
    return [lax.rem(me - k + count, count) for k in range(count)]


def power(exponent):
    return jnp.exp(exponent * math.log(2.0))


def exponent_of(peak):
    return jnp.ceil(jnp.log(jnp.maximum(peak, TINY)) * (1.0 / math.log(2.0)))


def filter_kernel(shards, rows, most, scale, packed, me_ref, *refs):
    u_refs = refs[:shards]
    g_refs = refs[shards : 2 * shards]
    ids_ref, ahead_ref, back_ref, out_ref, info_ref, u_all, g_all = refs[2 * shards :]
    length = shards * rows
    kernel = LANES

    @pl.when(pl.program_id(0) == 0)
    def _():
        documents(ids_ref, info_ref)
        u_all[:, :, length:, :] = jnp.zeros(u_all.shape[:2] + (most, LANES), jnp.float32)

    order = sources(me_ref[0], shards)
    wide = SUBS * BLOCK
    base = (me_ref[0] * pl.num_programs(0) + pl.program_id(0)) * wide
    ahead = ahead_ref[...]
    for sub in range(u_all.shape[0]):
        u_full, g_full = u_all.at[sub], g_all.at[sub]
        widen(u_refs, order, rows, u_full, sub, base)
        widen(g_refs, order, rows, g_full, sub, base)
        product = None
        for doc in range(DOCS):
            begin = info_ref[doc]
            g_wave = spectrum(ahead, window(g_full, begin, most, info_ref[DOCS + doc]))
            u_wave = spectrum(ahead, window(u_full, begin, most))
            more = against(g_wave, u_wave)
            product = more if product is None else [old + new for old, new in zip(product, more)]
        taps = inverse(back_ref[:kernel, :], product) * scale
        if packed:
            exponent = exponent_of(jnp.max(jnp.abs(taps), axis=0, keepdims=True))
            taps = taps * power(TOP - exponent)
        for tile in range(TILES):
            at = tile * LANES
            if packed:
                slot = (pl.program_id(0) * SUBS + sub) * TILES + tile
                out_ref[slot, :kernel, :] = taps[:, at : at + LANES]
                out_ref[slot, kernel:, :] = jnp.broadcast_to(exponent[:, at : at + LANES], (NOTE, LANES))
            else:
                out_ref[sub * BLOCK + at : sub * BLOCK + at + LANES, :] = taps[:, at : at + LANES].T


def grad_kernel(shards, rows, most, me_ref, *refs):
    g_refs = refs[:shards]
    ids_ref, ahead_ref, head_ref, back_ref, taps_ref, skip_ref = refs[shards : shards + 6]
    out_refs = refs[shards + 6 : 2 * shards + 6]
    info_ref, g_all, total_all = refs[2 * shards + 6 :]

    @pl.when(pl.program_id(0) == 0)
    def _():
        documents(ids_ref, info_ref)

    order = sources(me_ref[0], shards)
    wide = SUBS * BLOCK
    base = (me_ref[0] * pl.num_programs(0) + pl.program_id(0)) * wide
    ahead = ahead_ref[...]
    for sub in range(g_all.shape[0]):
        g_full, total_ref = g_all.at[sub], total_all.at[sub]
        widen(g_refs, order, rows, g_full, sub, base)
        taps = taps_ref[sub * BLOCK : (sub + 1) * BLOCK, :]
        h_wave = lax.dot_general(
            head_ref[...],
            jnp.concatenate([taps, taps], axis=1),
            (((1,), (1,)), ((), ())),
            preferred_element_type=jnp.float32,
        )
        for doc in range(DOCS):
            begin = info_ref[doc]
            g_wave = spectrum(ahead, window(g_full, begin, most, info_ref[DOCS + doc]))
            total = inverse(back_ref[...], against(g_wave, h_wave))
            for tile in range(TILES):
                for i in range(0, most, STEP):
                    total_ref[tile, pl.ds(begin + i, STEP), :] = total[i : i + STEP, tile * LANES : (tile + 1) * LANES]
        for out_ref, shard in zip(out_refs, order):
            at = pl.multiple_of(shard * rows, STEP)
            for tile in range(TILES):
                first = sub * BLOCK + tile * LANES
                lanes = slice(first, first + LANES)
                skipped = g_full[tile, pl.ds(at, rows), :] * skip_ref[:, lanes]
                out_ref[0, :, lanes] = (total_ref[tile, pl.ds(at, rows), :] + skipped).astype(out_ref.dtype)


def filter_part(me, u_list, g_list, ids, kernel, scale, width, packed):
    shards = len(u_list)
    rows = u_list[0].shape[1]
    length = shards * rows
    most = length // 2
    wide = SUBS * BLOCK
    blocks = width // wide
    ahead, back = tables(most, kernel)
    data = pl.BlockSpec((1, rows, wide), lambda c, me_ref: (0, 0, me_ref[0] * blocks + c))
    got = pl.BlockSpec(memory_space=pltpu.VMEM)
    fixed = lambda array: pl.BlockSpec(array.shape, lambda c, me_ref: (0, 0))
    if packed:
        shape = (width // LANES, kernel + NOTE, LANES)
        out_spec = pl.BlockSpec(memory_space=pltpu.VMEM)
        out_type = pltpu.VMEM(shape, jnp.float32)
    else:
        shape = (width, kernel)
        out_type = jax.ShapeDtypeStruct(shape, jnp.float32)
        out_spec = pl.BlockSpec((wide, kernel), lambda c, me_ref: (c, 0))
    return pl.pallas_call(
        functools.partial(filter_kernel, shards, rows, most, scale, packed),
        out_shape=out_type,
        grid_spec=pltpu.PrefetchScalarGridSpec(
            num_scalar_prefetch=1,
            grid=(blocks,),
            in_specs=([data] + [got] * (shards - 1)) * 2 + [fixed(ids), fixed(ahead), fixed(back)],
            out_specs=out_spec,
            scratch_shapes=[
                pltpu.SMEM((2 * DOCS,), jnp.int32),
                pltpu.VMEM((SUBS, TILES, length + most, LANES), jnp.float32),
                pltpu.VMEM((SUBS, TILES, length + most, LANES), jnp.float32),
            ],
        ),
        cost_estimate=pl.CostEstimate(
            flops=2 * width * (2 * DOCS * ahead.size + kernel * back.shape[1]),
            bytes_accessed=width * (4 * length + 4 * kernel),
            transcendentals=0,
        ),
    )(me, *u_list, *g_list, ids, jnp.asarray(ahead), jnp.asarray(back))


def grad_part(me, g_list, ids, taps, skip_gain, width):
    shards = len(g_list)
    rows = g_list[0].shape[1]
    kernel = taps.shape[1]
    length = shards * rows
    most = length // 2
    wide = SUBS * BLOCK
    blocks = width // wide
    ahead, back = tables(most, kernel)
    head = np.concatenate([ahead[:, :kernel], ahead[:, most : most + kernel]], axis=1)
    data = pl.BlockSpec((1, rows, wide), lambda c, me_ref: (0, 0, me_ref[0] * blocks + c))
    got = pl.BlockSpec(memory_space=pltpu.VMEM)
    fixed = lambda array: pl.BlockSpec(array.shape, lambda c, me_ref: (0, 0))
    return pl.pallas_call(
        functools.partial(grad_kernel, shards, rows, most),
        out_shape=[jax.ShapeDtypeStruct((1, rows, width), jnp.bfloat16)] * shards,
        grid_spec=pltpu.PrefetchScalarGridSpec(
            num_scalar_prefetch=1,
            grid=(blocks,),
            in_specs=[data] + [got] * (shards - 1)
            + [fixed(ids), fixed(ahead), fixed(head), fixed(back)]
            + [
                pl.BlockSpec((wide, kernel), lambda c, me_ref: (me_ref[0] * blocks + c, 0)),
                pl.BlockSpec((1, wide), lambda c, me_ref: (0, me_ref[0] * blocks + c)),
            ],
            out_specs=[pl.BlockSpec((1, rows, wide), lambda c, me_ref: (0, 0, c))] * shards,
            scratch_shapes=[
                pltpu.SMEM((2 * DOCS,), jnp.int32),
                pltpu.VMEM((SUBS, TILES, length + most, LANES), jnp.float32),
                pltpu.VMEM((SUBS, TILES, length + most, LANES), jnp.float32),
            ],
        ),
        cost_estimate=pl.CostEstimate(
            flops=2 * width * (DOCS * (ahead.size + back.size) + head.size),
            bytes_accessed=width * (4 * length + 2 * kernel),
            transcendentals=0,
        ),
    )(me, *g_list, ids, jnp.asarray(ahead), jnp.asarray(head), jnp.asarray(back), taps, skip_gain.reshape(1, -1))


def shifted(array, axis, count, step):
    return lax.ppermute(array, axis, [(i, (i + step) % count) for i in range(count)])


def exchanged(pieces, axis):
    return lax.all_to_all(pieces, axis, 0, 0, tiled=True)


def packed_sum(pieces):
    pieces = pieces.astype(jnp.float32)
    weights = power(pieces[:, LANES : LANES + 1, :] - TOP)
    total = jnp.sum(pieces[:, :LANES, :] * weights, axis=0)
    turned = total.T
    exponents = exponent_of(jnp.max(jnp.abs(turned), axis=0, keepdims=True))
    skip = total[:1, :] * power(TOP - exponents[:, :1])
    note = jnp.where(jnp.arange(NOTE)[:, None] == 0, exponents, skip)
    return jnp.concatenate([turned * power(TOP - exponents), note], axis=0)


def packed_whole(pieces):
    pieces = pieces.astype(jnp.float32)
    weights = power(pieces[:, LANES : LANES + 1, :] - TOP)
    whole = pieces[:, :LANES, :] * weights
    skip = pieces[:, LANES + 1, :] * weights[:, 0, :1]
    return whole.reshape(-1, whole.shape[2]), skip.reshape(-1)


def plain_sum(parts, axis, count):
    rows = up(parts.shape[0], count)
    padded = jnp.pad(parts, ((0, rows - parts.shape[0]), (0, 0)))
    piece = jnp.sum(exchanged(padded.reshape(count, rows // count, -1), axis), axis=0)
    whole = exchanged(jnp.broadcast_to(piece[None], (count,) + piece.shape), axis)
    whole = whole.reshape(rows, -1)[: parts.shape[0]]
    return whole, whole[:, 0]


def shards(inputs, cotangent, segment_ids, taps, skip_gain):
    count = lax.axis_size("ctx")
    groups = lax.axis_size("dp")
    me = lax.axis_index("ctx").astype(jnp.int32)[None]
    width = inputs.shape[2] // count
    kernel = taps.shape[1]
    scale = 1.0 / (inputs.shape[0] * groups)
    packed = width == groups * LANES and kernel == LANES
    held = lambda array: pltpu.with_memory_space_constraint(array, pltpu.VMEM) if packed else array
    u_list = [inputs] + [held(shifted(inputs, "ctx", count, k)) for k in range(1, count)]
    g_list = [cotangent] + [held(shifted(cotangent, "ctx", count, k)) for k in range(1, count)]
    parts = filter_part(me, u_list, g_list, segment_ids, kernel, scale, width, packed)
    if packed:
        pieces = exchanged(parts.astype(jnp.float16), "dp")
    grads = grad_part(me, g_list, segment_ids, taps, skip_gain, width)
    if packed:
        share = packed_sum(pieces)
        share = jnp.broadcast_to(share[None], (groups,) + share.shape).astype(jnp.float16)
        taps_grad, skip_grad = packed_whole(exchanged(share, "dp"))
    else:
        taps_grad, skip_grad = plain_sum(parts, "dp", groups)
    input_grad = jnp.zeros(inputs.shape, jnp.bfloat16)
    for k in range(count):
        got = grads[k] if k == 0 else shifted(grads[k], "ctx", count, -k)
        owner = lax.rem(me[0] + k, count)
        input_grad = lax.dynamic_update_slice(input_grad, got, (0, 0, owner * width))
    return input_grad, taps_grad, skip_grad


def solution(mesh):
    return jax.shard_map(
        shards,
        mesh=mesh,
        in_specs=(P("dp", "ctx", None), P("dp", "ctx", None), P("dp", None), P(), P()),
        out_specs=(P("dp", "ctx", None), P("ctx", None), P("ctx")),
        check_vma=False,
    )
```

```python
import functools
import math
import jax
import jax.numpy as jnp
import numpy as np
from jax import lax
from jax.experimental import pallas as pl
from jax.experimental.pallas import tpu as pltpu
from jax.sharding import PartitionSpec as P

LANES = 128
STEP = 8
TILES = 2
SUBS = 4
BLOCK = LANES * TILES
DOCS = 4
TOP = 12.0
NOTE = STEP
TINY = 1e-30


def up(value, unit):
    return -(-value // unit) * unit


def halves(table):
    high = np.asarray(table, np.float32).astype(jnp.bfloat16)
    low = (np.asarray(table, np.float64) - high.astype(np.float64)).astype(np.float32).astype(jnp.bfloat16)
    return high, low


def tables(most, kernel):
    period = most + kernel
    waves = period // 2
    angle = np.pi * np.outer(2 * np.arange(waves) + 1, np.arange(most)) / period
    pair = np.stack([np.cos(angle).reshape(-1, STEP, most), -np.sin(angle).reshape(-1, STEP, most)], axis=1)
    pair = pair.reshape(period, most)
    ahead = np.concatenate(halves(pair), axis=1)
    back = halves(pair.T / waves)
    back = np.concatenate([back[0], back[0], back[1]], axis=1)
    return ahead, back


def spectrum(table, value):
    return jnp.dot(table, jnp.concatenate([value, value], axis=0), preferred_element_type=jnp.float32)


def against(left, right):
    product = []
    for at in range(0, left.shape[0], 2 * STEP):
        lr, li = left[at : at + STEP], left[at + STEP : at + 2 * STEP]
        rr, ri = right[at : at + STEP], right[at + STEP : at + 2 * STEP]
        product += [lr * rr + li * ri, li * rr - lr * ri]
    return product


def inverse(table, product):
    high, low = [], []
    for at in range(0, len(product), 2):
        value = jnp.concatenate(product[at : at + 2], axis=0)
        high.append(value.astype(jnp.bfloat16))
        low.append((value - high[-1].astype(jnp.float32)).astype(jnp.bfloat16))
    return jnp.dot(table, jnp.concatenate(high + low + high, axis=0), preferred_element_type=jnp.float32)


def documents(ids_ref, info_ref):
    ids = ids_ref[...]
    begin = jnp.int32(0)
    for doc in range(DOCS):
        count = jnp.sum(jnp.where(ids == doc, 1.0, 0.0)).astype(jnp.int32)
        info_ref[doc] = begin
        info_ref[DOCS + doc] = count
        begin = begin + count


def widen(refs, shards, rows, full_ref, sub, base):
    for k, (ref, shard) in enumerate(zip(refs, shards)):
        at = pl.multiple_of(shard * rows, STEP)
        for tile in range(TILES):
            first = sub * BLOCK + tile * LANES
            if k:
                first = pl.multiple_of(base + first, LANES)
            block = ref[0, :, pl.ds(first, LANES)]
            full_ref[tile, pl.ds(at, rows), :] = block.astype(jnp.float32)


def window(full_ref, begin, most, count=None):
    tiles = []
    for tile in range(TILES):
        column = [full_ref[tile, pl.ds(begin + i, STEP), :] for i in range(0, most, STEP)]
        tiles.append(jnp.concatenate(column, axis=0))
    value = jnp.concatenate(tiles, axis=1)
    if count is not None:
        value = jnp.where(lax.broadcasted_iota(jnp.int32, value.shape, 0) < count, value, 0.0)
    return value.astype(jnp.bfloat16)


def sources(me, count):
    return [lax.rem(me - k + count, count) for k in range(count)]


def power(exponent):
    return jnp.exp(exponent * math.log(2.0))


def exponent_of(peak):
    return jnp.ceil(jnp.log(jnp.maximum(peak, TINY)) * (1.0 / math.log(2.0)))


def filter_kernel(shards, rows, most, scale, packed, me_ref, *refs):
    u_refs = refs[:shards]
    g_refs = refs[shards : 2 * shards]
    ids_ref, ahead_ref, back_ref, out_ref, info_ref, u_all, g_all = refs[2 * shards :]
    length = shards * rows
    kernel = LANES

    @pl.when(pl.program_id(0) == 0)
    def _():
        documents(ids_ref, info_ref)
        u_all[:, :, length:, :] = jnp.zeros(u_all.shape[:2] + (most, LANES), jnp.float32)

    order = sources(me_ref[0], shards)
    wide = SUBS * BLOCK
    base = pl.program_id(0) * wide
    ahead = ahead_ref[...]
    for sub in range(u_all.shape[0]):
        u_full, g_full = u_all.at[sub], g_all.at[sub]
        widen(u_refs, order, rows, u_full, sub, base)
        widen(g_refs, order, rows, g_full, sub, base)
        product = None
        for doc in range(DOCS):
            begin = info_ref[doc]
            g_wave = spectrum(ahead, window(g_full, begin, most, info_ref[DOCS + doc]))
            u_wave = spectrum(ahead, window(u_full, begin, most))
            more = against(g_wave, u_wave)
            product = more if product is None else [old + new for old, new in zip(product, more)]
        taps = inverse(back_ref[:kernel, :], product) * scale
        if packed:
            exponent = exponent_of(jnp.max(jnp.abs(taps), axis=0, keepdims=True))
            taps = taps * power(TOP - exponent)
        for tile in range(TILES):
            at = tile * LANES
            if packed:
                slot = (pl.program_id(0) * SUBS + sub) * TILES + tile
                out_ref[slot, :kernel, :] = taps[:, at : at + LANES]
                out_ref[slot, kernel:, :] = jnp.broadcast_to(exponent[:, at : at + LANES], (NOTE, LANES))
            else:
                out_ref[sub * BLOCK + at : sub * BLOCK + at + LANES, :] = taps[:, at : at + LANES].T


def grad_kernel(shards, rows, most, me_ref, *refs):
    g_refs = refs[:shards]
    ids_ref, ahead_ref, head_ref, back_ref, taps_ref, skip_ref = refs[shards : shards + 6]
    out_refs = refs[shards + 6 : 2 * shards + 6]
    info_ref, g_all, total_all = refs[2 * shards + 6 :]

    @pl.when(pl.program_id(0) == 0)
    def _():
        documents(ids_ref, info_ref)

    order = sources(me_ref[0], shards)
    wide = SUBS * BLOCK
    base = pl.program_id(0) * wide
    ahead = ahead_ref[...]
    for sub in range(g_all.shape[0]):
        g_full, total_ref = g_all.at[sub], total_all.at[sub]
        widen(g_refs, order, rows, g_full, sub, base)
        taps = taps_ref[sub * BLOCK : (sub + 1) * BLOCK, :]
        h_wave = lax.dot_general(
            head_ref[...],
            jnp.concatenate([taps, taps], axis=1),
            (((1,), (1,)), ((), ())),
            preferred_element_type=jnp.float32,
        )
        for doc in range(DOCS):
            begin = info_ref[doc]
            g_wave = spectrum(ahead, window(g_full, begin, most, info_ref[DOCS + doc]))
            total = inverse(back_ref[...], against(g_wave, h_wave))
            for tile in range(TILES):
                for i in range(0, most, STEP):
                    total_ref[tile, pl.ds(begin + i, STEP), :] = total[i : i + STEP, tile * LANES : (tile + 1) * LANES]
        for out_ref, shard in zip(out_refs, order):
            at = pl.multiple_of(shard * rows, STEP)
            for tile in range(TILES):
                first = sub * BLOCK + tile * LANES
                lanes = slice(first, first + LANES)
                skipped = g_full[tile, pl.ds(at, rows), :] * skip_ref[:, lanes]
                out_ref[0, :, lanes] = (total_ref[tile, pl.ds(at, rows), :] + skipped).astype(out_ref.dtype)


def filter_part(me, u_list, g_list, ids, kernel, scale, width, packed):
    shards = len(u_list)
    rows = u_list[0].shape[1]
    length = shards * rows
    most = length // 2
    wide = SUBS * BLOCK
    blocks = width // wide
    ahead, back = tables(most, kernel)
    data = pl.BlockSpec((1, rows, wide), lambda c, me_ref: (0, 0, me_ref[0] * blocks + c))
    got = pl.BlockSpec(memory_space=pltpu.VMEM)
    fixed = lambda array: pl.BlockSpec(array.shape, lambda c, me_ref: (0, 0))
    if packed:
        shape = (width // LANES, kernel + NOTE, LANES)
        out_spec = pl.BlockSpec(memory_space=pltpu.VMEM)
        out_type = pltpu.VMEM(shape, jnp.float32)
    else:
        shape = (width, kernel)
        out_type = jax.ShapeDtypeStruct(shape, jnp.float32)
        out_spec = pl.BlockSpec((wide, kernel), lambda c, me_ref: (c, 0))
    return pl.pallas_call(
        functools.partial(filter_kernel, shards, rows, most, scale, packed),
        out_shape=out_type,
        grid_spec=pltpu.PrefetchScalarGridSpec(
            num_scalar_prefetch=1,
            grid=(blocks,),
            in_specs=([data] + [got] * (shards - 1)) * 2 + [fixed(ids), fixed(ahead), fixed(back)],
            out_specs=out_spec,
            scratch_shapes=[
                pltpu.SMEM((2 * DOCS,), jnp.int32),
                pltpu.VMEM((SUBS, TILES, length + most, LANES), jnp.float32),
                pltpu.VMEM((SUBS, TILES, length + most, LANES), jnp.float32),
            ],
        ),
        cost_estimate=pl.CostEstimate(
            flops=2 * width * (2 * DOCS * ahead.size + kernel * back.shape[1]),
            bytes_accessed=width * (4 * length + 4 * kernel),
            transcendentals=0,
        ),
    )(me, *u_list, *g_list, ids, jnp.asarray(ahead), jnp.asarray(back))


def grad_part(me, g_list, ids, taps, skip_gain, width):
    shards = len(g_list)
    rows = g_list[0].shape[1]
    kernel = taps.shape[1]
    length = shards * rows
    most = length // 2
    wide = SUBS * BLOCK
    blocks = width // wide
    ahead, back = tables(most, kernel)
    head = np.concatenate([ahead[:, :kernel], ahead[:, most : most + kernel]], axis=1)
    data = pl.BlockSpec((1, rows, wide), lambda c, me_ref: (0, 0, me_ref[0] * blocks + c))
    got = pl.BlockSpec(memory_space=pltpu.VMEM)
    fixed = lambda array: pl.BlockSpec(array.shape, lambda c, me_ref: (0, 0))
    return pl.pallas_call(
        functools.partial(grad_kernel, shards, rows, most),
        out_shape=[jax.ShapeDtypeStruct((1, rows, width), jnp.bfloat16)] * shards,
        grid_spec=pltpu.PrefetchScalarGridSpec(
            num_scalar_prefetch=1,
            grid=(blocks,),
            in_specs=[data] + [got] * (shards - 1)
            + [fixed(ids), fixed(ahead), fixed(head), fixed(back)]
            + [
                pl.BlockSpec((wide, kernel), lambda c, me_ref: (me_ref[0] * blocks + c, 0)),
                pl.BlockSpec((1, wide), lambda c, me_ref: (0, me_ref[0] * blocks + c)),
            ],
            out_specs=[pl.BlockSpec((1, rows, wide), lambda c, me_ref: (0, 0, c))] * shards,
            scratch_shapes=[
                pltpu.SMEM((2 * DOCS,), jnp.int32),
                pltpu.VMEM((SUBS, TILES, length + most, LANES), jnp.float32),
                pltpu.VMEM((SUBS, TILES, length + most, LANES), jnp.float32),
            ],
        ),
        cost_estimate=pl.CostEstimate(
            flops=2 * width * (DOCS * (ahead.size + back.size) + head.size),
            bytes_accessed=width * (4 * length + 2 * kernel),
            transcendentals=0,
        ),
    )(me, *g_list, ids, jnp.asarray(ahead), jnp.asarray(head), jnp.asarray(back), taps, skip_gain.reshape(1, -1))


def shifted(array, axis, count, step):
    return lax.ppermute(array, axis, [(i, (i + step) % count) for i in range(count)])


def exchanged(pieces, axis):
    return lax.all_to_all(pieces, axis, 0, 0, tiled=True)


def packed_sum(pieces):
    pieces = pieces.astype(jnp.float32)
    weights = power(pieces[:, LANES : LANES + 1, :] - TOP)
    total = jnp.sum(pieces[:, :LANES, :] * weights, axis=0)
    turned = total.T
    exponents = exponent_of(jnp.max(jnp.abs(turned), axis=0, keepdims=True))
    skip = total[:1, :] * power(TOP - exponents[:, :1])
    note = jnp.where(jnp.arange(NOTE)[:, None] == 0, exponents, skip)
    return jnp.concatenate([turned * power(TOP - exponents), note], axis=0)


def whole_kernel(pieces_ref, taps_ref, skip_ref):
    for k in range(pieces_ref.shape[0]):
        note = pieces_ref[k, LANES:, :]
        weights = power(note[:1] - TOP)
        taps_ref[k * LANES : (k + 1) * LANES, :] = pieces_ref[k, :LANES, :] * weights
        skip_ref[k : k + 1, :] = note[1:2] * weights[:, :1]


def packed_whole(pieces):
    pieces = pltpu.with_memory_space_constraint(pieces.astype(jnp.float32), pltpu.VMEM)
    count = pieces.shape[0]
    whole, skip = pl.pallas_call(
        whole_kernel,
        grid=(count // STEP,),
        in_specs=[pl.BlockSpec((STEP,) + pieces.shape[1:], lambda c: (c, 0, 0), memory_space=pltpu.VMEM)],
        out_specs=[pl.BlockSpec((STEP * LANES, LANES), lambda c: (c, 0)), pl.BlockSpec((STEP, LANES), lambda c: (c, 0))],
        out_shape=[
            jax.ShapeDtypeStruct((count * LANES, LANES), jnp.float32),
            jax.ShapeDtypeStruct((count, LANES), jnp.float32),
        ],
    )(pieces)
    return whole, skip.reshape(-1)


def plain_sum(parts, axis, count):
    rows = up(parts.shape[0], count)
    padded = jnp.pad(parts, ((0, rows - parts.shape[0]), (0, 0)))
    piece = jnp.sum(exchanged(padded.reshape(count, rows // count, -1), axis), axis=0)
    whole = exchanged(jnp.broadcast_to(piece[None], (count,) + piece.shape), axis)
    whole = whole.reshape(rows, -1)[: parts.shape[0]]
    return whole, whole[:, 0]


def shards(inputs, cotangent, segment_ids, taps, skip_gain):
    count = lax.axis_size("ctx")
    groups = lax.axis_size("dp")
    me = lax.axis_index("ctx").astype(jnp.int32)[None]
    width = inputs.shape[2] // count
    kernel = taps.shape[1]
    scale = 1.0 / (inputs.shape[0] * groups)
    packed = width == groups * LANES and kernel == LANES and groups % STEP == 0
    held = lambda array: pltpu.with_memory_space_constraint(array, pltpu.VMEM) if packed else array

    def wanted(array, step):
        first = lax.rem(me[0] + step, count) * width
        return held(shifted(lax.dynamic_slice_in_dim(array, first, width, 2), "ctx", count, step))

    u_list = [inputs] + [wanted(inputs, k) for k in range(1, count)]
    g_list = [cotangent] + [wanted(cotangent, k) for k in range(1, count)]
    parts = filter_part(me, u_list, g_list, segment_ids, kernel, scale, width, packed)
    if packed:
        pieces = exchanged(parts.astype(jnp.float16), "dp")
    grads = grad_part(me, g_list, segment_ids, taps, skip_gain, width)
    if packed:
        share = packed_sum(pieces)
        share = jnp.broadcast_to(share[None], (groups,) + share.shape).astype(jnp.float16)
        taps_grad, skip_grad = packed_whole(exchanged(share, "dp"))
    else:
        taps_grad, skip_grad = plain_sum(parts, "dp", groups)
    input_grad = jnp.zeros(inputs.shape, jnp.bfloat16)
    for k in range(count):
        got = grads[k] if k == 0 else shifted(grads[k], "ctx", count, -k)
        owner = lax.rem(me[0] + k, count)
        input_grad = lax.dynamic_update_slice(input_grad, got, (0, 0, owner * width))
    return input_grad, taps_grad, skip_grad


def solution(mesh):
    return jax.shard_map(
        shards,
        mesh=mesh,
        in_specs=(P("dp", "ctx", None), P("dp", "ctx", None), P("dp", None), P(), P()),
        out_specs=(P("dp", "ctx", None), P("ctx", None), P("ctx")),
        check_vma=False,
    )
```

```python
import functools
import math
import jax
import jax.numpy as jnp
import numpy as np
from jax import lax
from jax.experimental import pallas as pl
from jax.experimental.pallas import tpu as pltpu
from jax.sharding import PartitionSpec as P

LANES = 128
STEP = 8
TILES = 2
SUBS = 4
BLOCK = LANES * TILES
DOCS = 4
TOP = 12.0
NOTE = STEP
TINY = 1e-30
LONG = 2


def up(value, unit):
    return -(-value // unit) * unit


def halves(table):
    high = np.asarray(table, np.float32).astype(jnp.bfloat16)
    low = (np.asarray(table, np.float64) - high.astype(np.float64)).astype(np.float32).astype(jnp.bfloat16)
    return high, low


def tables(most, kernel):
    period = most + kernel
    waves = period // 2
    angle = np.pi * np.outer(2 * np.arange(waves) + 1, np.arange(most)) / period
    pair = np.stack([np.cos(angle).reshape(-1, STEP, most), -np.sin(angle).reshape(-1, STEP, most)], axis=1)
    pair = pair.reshape(period, most)
    ahead = np.concatenate(halves(pair), axis=1)
    back = halves(pair.T / waves)
    back = np.concatenate([back[0], back[0], back[1]], axis=1)
    return ahead, back


def spectrum(table, value):
    return jnp.dot(table, jnp.concatenate([value, value], axis=0), preferred_element_type=jnp.float32)


def against(left, right):
    product = []
    for at in range(0, left.shape[0], 2 * STEP):
        lr, li = left[at : at + STEP], left[at + STEP : at + 2 * STEP]
        rr, ri = right[at : at + STEP], right[at + STEP : at + 2 * STEP]
        product += [lr * rr + li * ri, li * rr - lr * ri]
    return product


def inverse(table, product):
    high, low = [], []
    for at in range(0, len(product), 2):
        value = jnp.concatenate(product[at : at + 2], axis=0)
        high.append(value.astype(jnp.bfloat16))
        low.append((value - high[-1].astype(jnp.float32)).astype(jnp.bfloat16))
    return jnp.dot(table, jnp.concatenate(high + low + high, axis=0), preferred_element_type=jnp.float32)


def documents(ids_ref, info_ref, ranked=False):
    ids = ids_ref[...]
    begin = jnp.int32(0)
    begins, counts = [], []
    for doc in range(DOCS):
        count = jnp.sum(jnp.where(ids == doc, 1.0, 0.0)).astype(jnp.int32)
        begins.append(begin)
        counts.append(count)
        begin = begin + count
    for doc in range(DOCS):
        slot = doc
        if ranked:
            ahead = [counts[k] >= counts[doc] if k < doc else counts[k] > counts[doc] for k in range(DOCS) if k != doc]
            slot = sum(jnp.where(flag, 1, 0) for flag in ahead)
        info_ref[slot] = begins[doc]
        info_ref[DOCS + slot] = counts[doc]


def widen(refs, shards, rows, full_ref, sub, base):
    for k, (ref, shard) in enumerate(zip(refs, shards)):
        at = pl.multiple_of(shard * rows, STEP)
        for tile in range(TILES):
            first = sub * BLOCK + tile * LANES
            if k:
                first = pl.multiple_of(base + first, LANES)
            block = ref[0, :, pl.ds(first, LANES)]
            full_ref[tile, pl.ds(at, rows), :] = block.astype(jnp.float32)


def window(full_ref, begin, most, count=None):
    tiles = []
    for tile in range(TILES):
        column = [full_ref[tile, pl.ds(begin + i, STEP), :] for i in range(0, most, STEP)]
        tiles.append(jnp.concatenate(column, axis=0))
    value = jnp.concatenate(tiles, axis=1)
    if count is not None:
        value = jnp.where(lax.broadcasted_iota(jnp.int32, value.shape, 0) < count, value, 0.0)
    return value.astype(jnp.bfloat16)


def sources(me, count):
    return [lax.rem(me - k + count, count) for k in range(count)]


def power(exponent):
    return jnp.exp(exponent * math.log(2.0))


def exponent_of(peak):
    return jnp.ceil(jnp.log(jnp.maximum(peak, TINY)) * (1.0 / math.log(2.0)))


def filter_kernel(shards, rows, most, scale, packed, me_ref, *refs):
    u_refs = refs[:shards]
    g_refs = refs[shards : 2 * shards]
    ids_ref, ahead_ref, back_ref, brief_ahead_ref, brief_back_ref = refs[2 * shards : 2 * shards + 5]
    out_ref, info_ref, u_all, g_all = refs[2 * shards + 5 :]
    length = shards * rows
    kernel = LANES

    @pl.when(pl.program_id(0) == 0)
    def _():
        documents(ids_ref, info_ref, ranked=True)
        u_all[:, :, length:, :] = jnp.zeros(u_all.shape[:2] + (most, LANES), jnp.float32)

    order = sources(me_ref[0], shards)
    wide = SUBS * BLOCK
    base = pl.program_id(0) * wide
    far = base + me_ref[0] * (pl.num_programs(0) * wide)
    for sub in range(u_all.shape[0]):
        u_full, g_full = u_all.at[sub], g_all.at[sub]
        widen(u_refs, order, rows, u_full, sub, base)
        widen(g_refs, order, rows, g_full, sub, far)
        taps = 0.0
        for slots, reach, ahead, back_at in (
            (range(LONG), most, ahead_ref[...], back_ref),
            (range(LONG, DOCS), most // 2, brief_ahead_ref[...], brief_back_ref),
        ):
            product = None
            for slot in slots:
                begin = info_ref[slot]
                g_wave = spectrum(ahead, window(g_full, begin, reach, info_ref[DOCS + slot]))
                u_wave = spectrum(ahead, window(u_full, begin, reach))
                more = against(g_wave, u_wave)
                product = more if product is None else [old + new for old, new in zip(product, more)]
            lags = min(kernel, reach)
            part = inverse(back_at[:lags, :], product)
            if lags < kernel:
                part = jnp.concatenate([part, jnp.zeros((kernel - lags, BLOCK), jnp.float32)], axis=0)
            taps = taps + part
        taps = taps * scale
        if packed:
            exponent = exponent_of(jnp.max(jnp.abs(taps), axis=0, keepdims=True))
            taps = taps * power(TOP - exponent)
        for tile in range(TILES):
            at = tile * LANES
            if packed:
                slot = (pl.program_id(0) * SUBS + sub) * TILES + tile
                out_ref[slot, :kernel, :] = taps[:, at : at + LANES]
                out_ref[slot, kernel:, :] = jnp.broadcast_to(exponent[:, at : at + LANES], (NOTE, LANES))
            else:
                out_ref[sub * BLOCK + at : sub * BLOCK + at + LANES, :] = taps[:, at : at + LANES].T


def grad_kernel(shards, rows, most, me_ref, *refs):
    g_refs = refs[:shards]
    ids_ref, ahead_ref, head_ref, back_ref, taps_ref, skip_ref = refs[shards : shards + 6]
    out_refs = refs[shards + 6 : 2 * shards + 6]
    info_ref, g_all, total_all = refs[2 * shards + 6 :]

    @pl.when(pl.program_id(0) == 0)
    def _():
        documents(ids_ref, info_ref)

    order = sources(me_ref[0], shards)
    wide = SUBS * BLOCK
    base = pl.program_id(0) * wide
    far = base + me_ref[0] * (pl.num_programs(0) * wide)
    ahead = ahead_ref[...]
    for sub in range(g_all.shape[0]):
        g_full, total_ref = g_all.at[sub], total_all.at[sub]
        widen(g_refs, order, rows, g_full, sub, far)
        taps = taps_ref[sub * BLOCK : (sub + 1) * BLOCK, :]
        h_wave = lax.dot_general(
            head_ref[...],
            jnp.concatenate([taps, taps], axis=1),
            (((1,), (1,)), ((), ())),
            preferred_element_type=jnp.float32,
        )
        for doc in range(DOCS):
            begin = info_ref[doc]
            g_wave = spectrum(ahead, window(g_full, begin, most, info_ref[DOCS + doc]))
            total = inverse(back_ref[...], against(g_wave, h_wave))
            for tile in range(TILES):
                for i in range(0, most, STEP):
                    total_ref[tile, pl.ds(begin + i, STEP), :] = total[i : i + STEP, tile * LANES : (tile + 1) * LANES]
        for out_ref, shard in zip(out_refs, order):
            at = pl.multiple_of(shard * rows, STEP)
            for tile in range(TILES):
                first = sub * BLOCK + tile * LANES
                lanes = slice(first, first + LANES)
                skipped = g_full[tile, pl.ds(at, rows), :] * skip_ref[:, lanes]
                out_ref[0, :, lanes] = (total_ref[tile, pl.ds(at, rows), :] + skipped).astype(out_ref.dtype)


def filter_part(me, u_list, g_list, ids, kernel, scale, width, packed):
    shards = len(u_list)
    rows = u_list[0].shape[1]
    length = shards * rows
    most = length // 2
    wide = SUBS * BLOCK
    blocks = width // wide
    fixed_tables = tables(most, kernel) + tables(most // 2, min(kernel, most // 2))
    ahead, back = fixed_tables[:2]
    data = pl.BlockSpec((1, rows, wide), lambda c, me_ref: (0, 0, me_ref[0] * blocks + c))
    got = pl.BlockSpec(memory_space=pltpu.VMEM)
    fixed = lambda array: pl.BlockSpec(array.shape, lambda c, me_ref: (0, 0))
    if packed:
        shape = (width // LANES, kernel + NOTE, LANES)
        out_spec = pl.BlockSpec(memory_space=pltpu.VMEM)
        out_type = pltpu.VMEM(shape, jnp.float32)
    else:
        shape = (width, kernel)
        out_type = jax.ShapeDtypeStruct(shape, jnp.float32)
        out_spec = pl.BlockSpec((wide, kernel), lambda c, me_ref: (c, 0))
    return pl.pallas_call(
        functools.partial(filter_kernel, shards, rows, most, scale, packed),
        out_shape=out_type,
        grid_spec=pltpu.PrefetchScalarGridSpec(
            num_scalar_prefetch=1,
            grid=(blocks,),
            in_specs=([data] + [got] * (shards - 1)) * 2 + [fixed(ids)] + [fixed(table) for table in fixed_tables],
            out_specs=out_spec,
            scratch_shapes=[
                pltpu.SMEM((2 * DOCS,), jnp.int32),
                pltpu.VMEM((SUBS, TILES, length + most, LANES), jnp.float32),
                pltpu.VMEM((SUBS, TILES, length + most, LANES), jnp.float32),
            ],
        ),
        cost_estimate=pl.CostEstimate(
            flops=2 * width * (2 * DOCS * ahead.size + kernel * back.shape[1]),
            bytes_accessed=width * (4 * length + 4 * kernel),
            transcendentals=0,
        ),
    )(me, *u_list, *g_list, ids, *map(jnp.asarray, fixed_tables))


def grad_part(me, g_list, ids, taps, skip_gain, width):
    shards = len(g_list)
    rows = g_list[0].shape[1]
    kernel = taps.shape[1]
    length = shards * rows
    most = length // 2
    wide = SUBS * BLOCK
    blocks = width // wide
    ahead, back = tables(most, kernel)
    head = np.concatenate([ahead[:, :kernel], ahead[:, most : most + kernel]], axis=1)
    data = pl.BlockSpec((1, rows, wide), lambda c, me_ref: (0, 0, me_ref[0] * blocks + c))
    got = pl.BlockSpec(memory_space=pltpu.VMEM)
    fixed = lambda array: pl.BlockSpec(array.shape, lambda c, me_ref: (0, 0))
    return pl.pallas_call(
        functools.partial(grad_kernel, shards, rows, most),
        out_shape=[jax.ShapeDtypeStruct((1, rows, width), jnp.bfloat16)] * shards,
        grid_spec=pltpu.PrefetchScalarGridSpec(
            num_scalar_prefetch=1,
            grid=(blocks,),
            in_specs=[data] + [got] * (shards - 1)
            + [fixed(ids), fixed(ahead), fixed(head), fixed(back)]
            + [
                pl.BlockSpec((wide, kernel), lambda c, me_ref: (me_ref[0] * blocks + c, 0)),
                pl.BlockSpec((1, wide), lambda c, me_ref: (0, me_ref[0] * blocks + c)),
            ],
            out_specs=[pl.BlockSpec((1, rows, wide), lambda c, me_ref: (0, 0, c))] * shards,
            scratch_shapes=[
                pltpu.SMEM((2 * DOCS,), jnp.int32),
                pltpu.VMEM((SUBS, TILES, length + most, LANES), jnp.float32),
                pltpu.VMEM((SUBS, TILES, length + most, LANES), jnp.float32),
            ],
        ),
        cost_estimate=pl.CostEstimate(
            flops=2 * width * (DOCS * (ahead.size + back.size) + head.size),
            bytes_accessed=width * (4 * length + 2 * kernel),
            transcendentals=0,
        ),
    )(me, *g_list, ids, jnp.asarray(ahead), jnp.asarray(head), jnp.asarray(back), taps, skip_gain.reshape(1, -1))


def shifted(array, axis, count, step):
    return lax.ppermute(array, axis, [(i, (i + step) % count) for i in range(count)])


def exchanged(pieces, axis):
    return lax.all_to_all(pieces, axis, 0, 0, tiled=True)


def packed_sum(pieces):
    pieces = pieces.astype(jnp.float32)
    weights = power(pieces[:, LANES : LANES + 1, :] - TOP)
    total = jnp.sum(pieces[:, :LANES, :] * weights, axis=0)
    turned = total.T
    exponents = exponent_of(jnp.max(jnp.abs(turned), axis=0, keepdims=True))
    skip = total[:1, :] * power(TOP - exponents[:, :1])
    note = jnp.where(jnp.arange(NOTE)[:, None] == 0, exponents, skip)
    return jnp.concatenate([turned * power(TOP - exponents), note], axis=0)


def whole_kernel(pieces_ref, taps_ref, skip_ref):
    for k in range(pieces_ref.shape[0]):
        note = pieces_ref[k, LANES:, :]
        weights = power(note[:1] - TOP)
        taps_ref[k * LANES : (k + 1) * LANES, :] = pieces_ref[k, :LANES, :] * weights
        skip_ref[k : k + 1, :] = note[1:2] * weights[:, :1]


def packed_whole(pieces):
    pieces = pltpu.with_memory_space_constraint(pieces.astype(jnp.float32), pltpu.VMEM)
    count = pieces.shape[0]
    whole, skip = pl.pallas_call(
        whole_kernel,
        grid=(count // STEP,),
        in_specs=[pl.BlockSpec((STEP,) + pieces.shape[1:], lambda c: (c, 0, 0), memory_space=pltpu.VMEM)],
        out_specs=[pl.BlockSpec((STEP * LANES, LANES), lambda c: (c, 0)), pl.BlockSpec((STEP, LANES), lambda c: (c, 0))],
        out_shape=[
            jax.ShapeDtypeStruct((count * LANES, LANES), jnp.float32),
            jax.ShapeDtypeStruct((count, LANES), jnp.float32),
        ],
    )(pieces)
    return whole, skip.reshape(-1)


def plain_sum(parts, axis, count):
    rows = up(parts.shape[0], count)
    padded = jnp.pad(parts, ((0, rows - parts.shape[0]), (0, 0)))
    piece = jnp.sum(exchanged(padded.reshape(count, rows // count, -1), axis), axis=0)
    whole = exchanged(jnp.broadcast_to(piece[None], (count,) + piece.shape), axis)
    whole = whole.reshape(rows, -1)[: parts.shape[0]]
    return whole, whole[:, 0]


def shards(inputs, cotangent, segment_ids, taps, skip_gain):
    count = lax.axis_size("ctx")
    groups = lax.axis_size("dp")
    me = lax.axis_index("ctx").astype(jnp.int32)[None]
    width = inputs.shape[2] // count
    kernel = taps.shape[1]
    scale = 1.0 / (inputs.shape[0] * groups)
    packed = width == groups * LANES and kernel == LANES and groups % STEP == 0
    held = lambda array: pltpu.with_memory_space_constraint(array, pltpu.VMEM) if packed else array

    def wanted(array, step):
        first = lax.rem(me[0] + step, count) * width
        return held(shifted(lax.dynamic_slice_in_dim(array, first, width, 2), "ctx", count, step))

    u_list = [inputs] + [wanted(inputs, k) for k in range(1, count)]
    g_list = [cotangent] + [held(shifted(cotangent, "ctx", count, k)) for k in range(1, count)]
    parts = filter_part(me, u_list, g_list, segment_ids, kernel, scale, width, packed)
    if packed:
        pieces = exchanged(parts.astype(jnp.float16), "dp")
    grads = grad_part(me, g_list, segment_ids, taps, skip_gain, width)
    if packed:
        share = packed_sum(pieces)
        share = jnp.broadcast_to(share[None], (groups,) + share.shape).astype(jnp.float16)
        taps_grad, skip_grad = packed_whole(exchanged(share, "dp"))
    else:
        taps_grad, skip_grad = plain_sum(parts, "dp", groups)
    input_grad = jnp.zeros(inputs.shape, jnp.bfloat16)
    for k in range(count):
        got = grads[k] if k == 0 else shifted(grads[k], "ctx", count, -k)
        owner = lax.rem(me[0] + k, count)
        input_grad = lax.dynamic_update_slice(input_grad, got, (0, 0, owner * width))
    return input_grad, taps_grad, skip_grad


def solution(mesh):
    return jax.shard_map(
        shards,
        mesh=mesh,
        in_specs=(P("dp", "ctx", None), P("dp", "ctx", None), P("dp", None), P(), P()),
        out_specs=(P("dp", "ctx", None), P("ctx", None), P("ctx")),
        check_vma=False,
    )
```

```python
import functools
import math
import jax
import jax.numpy as jnp
import numpy as np
from jax import lax
from jax.experimental import pallas as pl
from jax.experimental.pallas import tpu as pltpu
from jax.sharding import PartitionSpec as P

LANES = 128
STEP = 8
TILES = 2
SUBS = 4
BLOCK = LANES * TILES
DOCS = 4
TOP = 12.0
NOTE = STEP
TINY = 1e-30
LONG = 2


def up(value, unit):
    return -(-value // unit) * unit


def halves(table):
    high = np.asarray(table, np.float32).astype(jnp.bfloat16)
    low = (np.asarray(table, np.float64) - high.astype(np.float64)).astype(np.float32).astype(jnp.bfloat16)
    return high, low


def tables(most, kernel):
    period = most + kernel
    waves = period // 2
    angle = np.pi * np.outer(2 * np.arange(waves) + 1, np.arange(most)) / period
    pair = np.stack([np.cos(angle).reshape(-1, STEP, most), -np.sin(angle).reshape(-1, STEP, most)], axis=1)
    pair = pair.reshape(period, most)
    ahead = np.concatenate(halves(pair), axis=1)
    back = halves(pair.T / waves)
    back = np.concatenate([back[0], back[0], back[1]], axis=1)
    return ahead, back


def spectrum(table, value):
    return jnp.dot(table, jnp.concatenate([value, value], axis=0), preferred_element_type=jnp.float32)


def against(left, right):
    product = []
    for at in range(0, left.shape[0], 2 * STEP):
        lr, li = left[at : at + STEP], left[at + STEP : at + 2 * STEP]
        rr, ri = right[at : at + STEP], right[at + STEP : at + 2 * STEP]
        product += [lr * rr + li * ri, li * rr - lr * ri]
    return product


def inverse(table, product):
    high, low = [], []
    for at in range(0, len(product), 2):
        value = jnp.concatenate(product[at : at + 2], axis=0)
        high.append(value.astype(jnp.bfloat16))
        low.append((value - high[-1].astype(jnp.float32)).astype(jnp.bfloat16))
    return jnp.dot(table, jnp.concatenate(high + low + high, axis=0), preferred_element_type=jnp.float32)


def documents(ids_ref, info_ref, ranked=False):
    ids = ids_ref[...]
    begin = jnp.int32(0)
    begins, counts = [], []
    for doc in range(DOCS):
        count = jnp.sum(jnp.where(ids == doc, 1.0, 0.0)).astype(jnp.int32)
        begins.append(begin)
        counts.append(count)
        begin = begin + count
    for doc in range(DOCS):
        slot = doc
        if ranked:
            ahead = [counts[k] >= counts[doc] if k < doc else counts[k] > counts[doc] for k in range(DOCS) if k != doc]
            slot = sum(jnp.where(flag, 1, 0) for flag in ahead)
        info_ref[slot] = begins[doc]
        info_ref[DOCS + slot] = counts[doc]


def widen(refs, shards, rows, full_ref, sub, base):
    for k, (ref, shard) in enumerate(zip(refs, shards)):
        at = pl.multiple_of(shard * rows, STEP)
        for tile in range(TILES):
            first = sub * BLOCK + tile * LANES
            if k:
                first = pl.multiple_of(base + first, LANES)
            block = ref[0, :, pl.ds(first, LANES)]
            full_ref[tile, pl.ds(at, rows), :] = block.astype(jnp.float32)


def window(full_ref, begin, most, count=None):
    tiles = []
    for tile in range(TILES):
        column = [full_ref[tile, pl.ds(begin + i, STEP), :] for i in range(0, most, STEP)]
        tiles.append(jnp.concatenate(column, axis=0))
    value = jnp.concatenate(tiles, axis=1)
    if count is not None:
        value = jnp.where(lax.broadcasted_iota(jnp.int32, value.shape, 0) < count, value, 0.0)
    return value.astype(jnp.bfloat16)


def sources(me, count):
    return [lax.rem(me - k + count, count) for k in range(count)]


def power(exponent):
    return jnp.exp(exponent * math.log(2.0))


def exponent_of(peak):
    return jnp.ceil(jnp.log(jnp.maximum(peak, TINY)) * (1.0 / math.log(2.0)))


def filter_kernel(shards, rows, most, scale, packed, me_ref, *refs):
    u_refs = refs[:shards]
    g_refs = refs[shards : 2 * shards]
    ids_ref, ahead_ref, back_ref, brief_ahead_ref, brief_back_ref = refs[2 * shards : 2 * shards + 5]
    out_ref, info_ref, u_all, g_all = refs[2 * shards + 5 :]
    length = shards * rows
    kernel = LANES

    @pl.when(pl.program_id(0) == 0)
    def _():
        documents(ids_ref, info_ref, ranked=True)
        u_all[:, :, length:, :] = jnp.zeros(u_all.shape[:2] + (most, LANES), jnp.float32)

    order = sources(me_ref[0], shards)
    wide = SUBS * BLOCK
    base = pl.program_id(0) * wide
    far = base + me_ref[0] * (pl.num_programs(0) * wide)
    for sub in range(u_all.shape[0]):
        widen(u_refs, order, rows, u_all.at[sub], sub, base)
        widen(g_refs, order, rows, g_all.at[sub], sub, far)
    for sub in range(u_all.shape[0]):
        u_full, g_full = u_all.at[sub], g_all.at[sub]
        taps = 0.0
        for slots, reach, ahead, back_at in (
            (range(LONG), most, ahead_ref[...], back_ref),
            (range(LONG, DOCS), most // 2, brief_ahead_ref[...], brief_back_ref),
        ):
            product = None
            for slot in slots:
                begin = info_ref[slot]
                g_wave = spectrum(ahead, window(g_full, begin, reach, info_ref[DOCS + slot]))
                u_wave = spectrum(ahead, window(u_full, begin, reach))
                more = against(g_wave, u_wave)
                product = more if product is None else [old + new for old, new in zip(product, more)]
            lags = min(kernel, reach)
            part = inverse(back_at[:lags, :], product)
            if lags < kernel:
                part = jnp.concatenate([part, jnp.zeros((kernel - lags, BLOCK), jnp.float32)], axis=0)
            taps = taps + part
        taps = taps * scale
        if packed:
            exponent = exponent_of(jnp.max(jnp.abs(taps), axis=0, keepdims=True))
            taps = taps * power(TOP - exponent)
        for tile in range(TILES):
            at = tile * LANES
            if packed:
                slot = (pl.program_id(0) * SUBS + sub) * TILES + tile
                out_ref[slot, :kernel, :] = taps[:, at : at + LANES]
                out_ref[slot, kernel:, :] = jnp.broadcast_to(exponent[:, at : at + LANES], (NOTE, LANES))
            else:
                out_ref[sub * BLOCK + at : sub * BLOCK + at + LANES, :] = taps[:, at : at + LANES].T


def grad_kernel(shards, rows, most, me_ref, *refs):
    g_refs = refs[:shards]
    ids_ref, ahead_ref, head_ref, back_ref, taps_ref, skip_ref = refs[shards : shards + 6]
    out_refs = refs[shards + 6 : 2 * shards + 6]
    info_ref, g_all, total_all = refs[2 * shards + 6 :]

    @pl.when(pl.program_id(0) == 0)
    def _():
        documents(ids_ref, info_ref)

    order = sources(me_ref[0], shards)
    wide = SUBS * BLOCK
    base = pl.program_id(0) * wide
    far = base + me_ref[0] * (pl.num_programs(0) * wide)
    ahead = ahead_ref[...]
    for sub in range(g_all.shape[0]):
        g_full, total_ref = g_all.at[sub], total_all.at[sub]
        widen(g_refs, order, rows, g_full, sub, far)
        taps = taps_ref[sub * BLOCK : (sub + 1) * BLOCK, :]
        h_wave = lax.dot_general(
            head_ref[...],
            jnp.concatenate([taps, taps], axis=1),
            (((1,), (1,)), ((), ())),
            preferred_element_type=jnp.float32,
        )
        for doc in range(DOCS):
            begin = info_ref[doc]
            g_wave = spectrum(ahead, window(g_full, begin, most, info_ref[DOCS + doc]))
            total = inverse(back_ref[...], against(g_wave, h_wave))
            for tile in range(TILES):
                for i in range(0, most, STEP):
                    total_ref[tile, pl.ds(begin + i, STEP), :] = total[i : i + STEP, tile * LANES : (tile + 1) * LANES]
        for out_ref, shard in zip(out_refs, order):
            at = pl.multiple_of(shard * rows, STEP)
            for tile in range(TILES):
                first = sub * BLOCK + tile * LANES
                lanes = slice(first, first + LANES)
                skipped = g_full[tile, pl.ds(at, rows), :] * skip_ref[:, lanes]
                out_ref[0, :, lanes] = (total_ref[tile, pl.ds(at, rows), :] + skipped).astype(out_ref.dtype)


def filter_part(me, u_list, g_list, ids, kernel, scale, width, packed):
    shards = len(u_list)
    rows = u_list[0].shape[1]
    length = shards * rows
    most = length // 2
    wide = SUBS * BLOCK
    blocks = width // wide
    fixed_tables = tables(most, kernel) + tables(most // 2, min(kernel, most // 2))
    ahead, back = fixed_tables[:2]
    data = pl.BlockSpec((1, rows, wide), lambda c, me_ref: (0, 0, me_ref[0] * blocks + c))
    got = pl.BlockSpec(memory_space=pltpu.VMEM)
    fixed = lambda array: pl.BlockSpec(array.shape, lambda c, me_ref: (0, 0))
    if packed:
        shape = (width // LANES, kernel + NOTE, LANES)
        out_spec = pl.BlockSpec(memory_space=pltpu.VMEM)
        out_type = pltpu.VMEM(shape, jnp.float32)
    else:
        shape = (width, kernel)
        out_type = jax.ShapeDtypeStruct(shape, jnp.float32)
        out_spec = pl.BlockSpec((wide, kernel), lambda c, me_ref: (c, 0))
    return pl.pallas_call(
        functools.partial(filter_kernel, shards, rows, most, scale, packed),
        out_shape=out_type,
        grid_spec=pltpu.PrefetchScalarGridSpec(
            num_scalar_prefetch=1,
            grid=(blocks,),
            in_specs=([data] + [got] * (shards - 1)) * 2 + [fixed(ids)] + [fixed(table) for table in fixed_tables],
            out_specs=out_spec,
            scratch_shapes=[
                pltpu.SMEM((2 * DOCS,), jnp.int32),
                pltpu.VMEM((SUBS, TILES, length + most, LANES), jnp.float32),
                pltpu.VMEM((SUBS, TILES, length + most, LANES), jnp.float32),
            ],
        ),
        cost_estimate=pl.CostEstimate(
            flops=2 * width * (2 * DOCS * ahead.size + kernel * back.shape[1]),
            bytes_accessed=width * (4 * length + 4 * kernel),
            transcendentals=0,
        ),
    )(me, *u_list, *g_list, ids, *map(jnp.asarray, fixed_tables))


def grad_part(me, g_list, ids, taps, skip_gain, width):
    shards = len(g_list)
    rows = g_list[0].shape[1]
    kernel = taps.shape[1]
    length = shards * rows
    most = length // 2
    wide = SUBS * BLOCK
    blocks = width // wide
    ahead, back = tables(most, kernel)
    head = np.concatenate([ahead[:, :kernel], ahead[:, most : most + kernel]], axis=1)
    data = pl.BlockSpec((1, rows, wide), lambda c, me_ref: (0, 0, me_ref[0] * blocks + c))
    got = pl.BlockSpec(memory_space=pltpu.VMEM)
    fixed = lambda array: pl.BlockSpec(array.shape, lambda c, me_ref: (0, 0))
    return pl.pallas_call(
        functools.partial(grad_kernel, shards, rows, most),
        out_shape=[jax.ShapeDtypeStruct((1, rows, width), jnp.bfloat16)] * shards,
        grid_spec=pltpu.PrefetchScalarGridSpec(
            num_scalar_prefetch=1,
            grid=(blocks,),
            in_specs=[data] + [got] * (shards - 1)
            + [fixed(ids), fixed(ahead), fixed(head), fixed(back)]
            + [
                pl.BlockSpec((wide, kernel), lambda c, me_ref: (me_ref[0] * blocks + c, 0)),
                pl.BlockSpec((1, wide), lambda c, me_ref: (0, me_ref[0] * blocks + c)),
            ],
            out_specs=[pl.BlockSpec((1, rows, wide), lambda c, me_ref: (0, 0, c))] * shards,
            scratch_shapes=[
                pltpu.SMEM((2 * DOCS,), jnp.int32),
                pltpu.VMEM((SUBS, TILES, length + most, LANES), jnp.float32),
                pltpu.VMEM((SUBS, TILES, length + most, LANES), jnp.float32),
            ],
        ),
        cost_estimate=pl.CostEstimate(
            flops=2 * width * (DOCS * (ahead.size + back.size) + head.size),
            bytes_accessed=width * (4 * length + 2 * kernel),
            transcendentals=0,
        ),
    )(me, *g_list, ids, jnp.asarray(ahead), jnp.asarray(head), jnp.asarray(back), taps, skip_gain.reshape(1, -1))


def shifted(array, axis, count, step):
    return lax.ppermute(array, axis, [(i, (i + step) % count) for i in range(count)])


def exchanged(pieces, axis):
    return lax.all_to_all(pieces, axis, 0, 0, tiled=True)


def packed_sum(pieces):
    pieces = pieces.astype(jnp.float32)
    weights = power(pieces[:, LANES : LANES + 1, :] - TOP)
    total = jnp.sum(pieces[:, :LANES, :] * weights, axis=0)
    turned = total.T
    exponents = exponent_of(jnp.max(jnp.abs(turned), axis=0, keepdims=True))
    skip = total[:1, :] * power(TOP - exponents[:, :1])
    note = jnp.where(jnp.arange(NOTE)[:, None] == 0, exponents, skip)
    return jnp.concatenate([turned * power(TOP - exponents), note], axis=0)


def whole_kernel(pieces_ref, taps_ref, skip_ref):
    for k in range(pieces_ref.shape[0]):
        note = pieces_ref[k, LANES:, :]
        weights = power(note[:1] - TOP)
        taps_ref[k * LANES : (k + 1) * LANES, :] = pieces_ref[k, :LANES, :] * weights
        skip_ref[k : k + 1, :] = note[1:2] * weights[:, :1]


def packed_whole(pieces):
    pieces = pltpu.with_memory_space_constraint(pieces.astype(jnp.float32), pltpu.VMEM)
    count = pieces.shape[0]
    whole, skip = pl.pallas_call(
        whole_kernel,
        grid=(count // STEP,),
        in_specs=[pl.BlockSpec((STEP,) + pieces.shape[1:], lambda c: (c, 0, 0), memory_space=pltpu.VMEM)],
        out_specs=[pl.BlockSpec((STEP * LANES, LANES), lambda c: (c, 0)), pl.BlockSpec((STEP, LANES), lambda c: (c, 0))],
        out_shape=[
            jax.ShapeDtypeStruct((count * LANES, LANES), jnp.float32),
            jax.ShapeDtypeStruct((count, LANES), jnp.float32),
        ],
    )(pieces)
    return whole, skip.reshape(-1)


def plain_sum(parts, axis, count):
    rows = up(parts.shape[0], count)
    padded = jnp.pad(parts, ((0, rows - parts.shape[0]), (0, 0)))
    piece = jnp.sum(exchanged(padded.reshape(count, rows // count, -1), axis), axis=0)
    whole = exchanged(jnp.broadcast_to(piece[None], (count,) + piece.shape), axis)
    whole = whole.reshape(rows, -1)[: parts.shape[0]]
    return whole, whole[:, 0]


def shards(inputs, cotangent, segment_ids, taps, skip_gain):
    count = lax.axis_size("ctx")
    groups = lax.axis_size("dp")
    me = lax.axis_index("ctx").astype(jnp.int32)[None]
    width = inputs.shape[2] // count
    kernel = taps.shape[1]
    scale = 1.0 / (inputs.shape[0] * groups)
    packed = width == groups * LANES and kernel == LANES and groups % STEP == 0
    held = lambda array: pltpu.with_memory_space_constraint(array, pltpu.VMEM) if packed else array

    def wanted(array, step):
        first = lax.rem(me[0] + step, count) * width
        return held(shifted(lax.dynamic_slice_in_dim(array, first, width, 2), "ctx", count, step))

    u_list = [inputs] + [wanted(inputs, k) for k in range(1, count)]
    g_list = [cotangent] + [held(shifted(cotangent, "ctx", count, k)) for k in range(1, count)]
    parts = filter_part(me, u_list, g_list, segment_ids, kernel, scale, width, packed)
    if packed:
        pieces = exchanged(parts.astype(jnp.float16), "dp")
    grads = grad_part(me, g_list, segment_ids, taps, skip_gain, width)
    if packed:
        share = packed_sum(pieces)
        share = jnp.broadcast_to(share[None], (groups,) + share.shape).astype(jnp.float16)
        taps_grad, skip_grad = packed_whole(exchanged(share, "dp"))
    else:
        taps_grad, skip_grad = plain_sum(parts, "dp", groups)
    input_grad = jnp.zeros(inputs.shape, jnp.bfloat16)
    for k in range(count):
        got = grads[k] if k == 0 else shifted(grads[k], "ctx", count, -k)
        owner = lax.rem(me[0] + k, count)
        input_grad = lax.dynamic_update_slice(input_grad, got, (0, 0, owner * width))
    return input_grad, taps_grad, skip_grad


def solution(mesh):
    return jax.shard_map(
        shards,
        mesh=mesh,
        in_specs=(P("dp", "ctx", None), P("dp", "ctx", None), P("dp", None), P(), P()),
        out_specs=(P("dp", "ctx", None), P("ctx", None), P("ctx")),
        check_vma=False,
    )
```
